1024 devices in a mesh: lat: 128 (over x, y, z_lo), lev: 8 (over z_hi, core).
Axes of the slice: x: 4, y: 8, z: 16 (z_hi: 4, z_lo: 4; z = z_hi * 4 + z_lo), core: 2. Of those that a mesh axis runs over, the one named last changes fastest.
Arguments:
- fields: float32 [3, 64, 256, 1024], P(None, 'lev', 'lat'), may hold values from -6 to 6
- north_courant: float32 [64, 256, 1024], P('lev', 'lat'), may hold values from 0.05 to 0.3
- south_courant: float32 [64, 256, 1024], P('lev', 'lat'), may hold values from 0.05 to 0.3
- east_courant: float32 [64, 256, 1024], P('lev', 'lat'), may hold values from 0.05 to 0.3
- limiter: int32 [64, 256, 1024], P('lev', 'lat'), may hold values from 0 to 3
- thickness: float32 [64, 256, 1024], P('lev', 'lat'), may hold values from 0.5 to 2
- sunlit: int32 [256, 8], P('lat', 'lev'), may hold values from 0 to 1, as said below
- absorb: float32 [2, 64], replicated, may hold values from 0.002 to 0.05
- solar_flux: float32 [64], replicated, may hold values from 0.1 to 1
Outputs:
- column_fields: float32 [3, 64, 256, 1024], P(None, None, 'lat', 'lev')
The draws below stay inside these ranges and needn't reach their ends.
Inputs may be any that keep to these rules, and one draw needn't show every extreme that they name: sunlit[r, b] + sunlit[(r + 128) mod 256, b] = 1 for every row r and block b: of two rows half the grid apart, exactly one is lit.
All inputs are finite; a program needn't handle non-finite values.
Results may differ from the reference program's by a relative error of at most 0.00019.
Values sent between devices are 32-bit elements; how exact they have to be, the bound alone decides.
No kernel may reach another device: no remote copies, remote signals or barrier semaphores. Data moves between devices by JAX's collectives and lax.ppermute only.
A program may use at most 32 MiB of HBM per device.

```python
import math
import jax
import jax.numpy as jnp
from jax import lax

LEVELS = 64
BAND_COUNT = 64
COLS_DEV = 128
GRID_ROWS = 256
GRID_COLS = 1024
COL_BLOCKS = 8


def draw_sunlit(key, part):
    half_rows = GRID_ROWS // 2
    picks = jax.random.randint(key, (half_rows, COL_BLOCKS), 0, half_rows)
    row_index = jnp.arange(half_rows, dtype=jnp.int32)[:, None]
    northern = (picks <= row_index).astype(jnp.int32)
    return jnp.concatenate([northern, 1 - northern], 0)


def set_ends(drawn, rng, least, high):
    place = [jax.random.randint(jax.random.fold_in(rng, axis), (), 0, length) for axis, length in enumerate(drawn.shape)]
    longest = drawn.shape.index(max(drawn.shape))
    neighbour = place[:longest] + [(place[longest] + 1) % drawn.shape[longest]] + place[longest + 1:]
    return drawn.at[tuple(place)].set(least).at[tuple(neighbour)].set(high)


def block_levels(rng, extent, split, low, largest):
    def one(axis_at, shards_of):
        heights = jax.random.uniform(jax.random.fold_in(jax.random.fold_in(rng, 6), axis_at), (shards_of,), jnp.float32, low / len(split), largest / len(split))
        return jnp.repeat(jnp.exp(heights), extent[axis_at] // shards_of).reshape((-1,) + (1,) * (len(extent) - axis_at - 1))

    factor_of = one(*split[0])
    for cut in split[1:]:
        factor_of = factor_of * one(*cut)
    return factor_of


def noise(own_key, shape, scale, most, shards=(), held_as=jnp.bfloat16):
    gain = block_levels(own_key, shape, shards, -0.22, 0.18) if shards else 1.0
    values = jax.random.normal(own_key, shape, jnp.float32) * scale * gain
    return jnp.minimum(jnp.maximum(values, -most), most).astype(held_as)


def setup_inputs(seed: int = 0) -> dict:
    keys = jax.random.split(jax.random.key(seed), 10)
    fields = noise(keys[0], (3, LEVELS, GRID_ROWS, GRID_COLS), 1.0, 6.0, ((1, 8), (2, 128)), jnp.float32)
    north_courant = jnp.clip(0.05 + 0.25 * jax.random.uniform(keys[1], (LEVELS, GRID_ROWS, GRID_COLS), jnp.float32) ** block_levels(keys[1], (LEVELS, GRID_ROWS, GRID_COLS), ((0, 8), (1, 128)), -0.2, 0.2), 0.05, 0.3)
    south_courant = jnp.clip(0.05 + 0.25 * jax.random.uniform(keys[2], (LEVELS, GRID_ROWS, GRID_COLS), jnp.float32) ** block_levels(keys[2], (LEVELS, GRID_ROWS, GRID_COLS), ((0, 8), (1, 128)), -0.2, 0.2), 0.05, 0.3)
    east_courant = jnp.clip(0.05 + 0.25 * jax.random.uniform(keys[3], (LEVELS, GRID_ROWS, GRID_COLS), jnp.float32) ** block_levels(keys[3], (LEVELS, GRID_ROWS, GRID_COLS), ((0, 8), (1, 128)), -0.2, 0.2), 0.05, 0.3)
    limiter = set_ends(jax.random.randint(keys[4], (LEVELS, GRID_ROWS, GRID_COLS), 0, 4), jax.random.fold_in(keys[4], 1), 0, 3).astype(jnp.int32)
    thickness = jnp.clip(0.5 + 1.5 * jax.random.uniform(keys[5], (LEVELS, GRID_ROWS, GRID_COLS), jnp.float32) ** block_levels(keys[5], (LEVELS, GRID_ROWS, GRID_COLS), ((0, 8), (1, 128)), -0.2, 0.2), 0.5, 2.0)
    sunlit = draw_sunlit(jax.random.fold_in(keys[9], 71), 0)
    absorb = jnp.clip(jnp.exp(jax.random.uniform(keys[7], (2, BAND_COUNT), jnp.float32, math.log(0.002), math.log(0.05))), 0.002, 0.05)
    solar_flux = jnp.clip(jnp.exp(jax.random.uniform(keys[8], (BAND_COUNT,), jnp.float32, math.log(0.1), math.log(1.0))), 0.1, 1.0)
    return {"fields": fields, "north_courant": north_courant, "south_courant": south_courant, "east_courant": east_courant, "limiter": limiter, "thickness": thickness, "sunlit": sunlit, "absorb": absorb, "solar_flux": solar_flux}


lw_rate = 0.2
lw_damp = 0.1


def pick_slope(limiter_code, back_diff, fore_diff):
    centred = 0.5 * (back_diff + fore_diff)
    return jnp.where(limiter_code == 1, back_diff, jnp.where(limiter_code == 2, fore_diff, jnp.where(limiter_code == 3, centred, jnp.zeros_like(centred))))


def face_fluxes(values, limiter_code, back_diff, fore_diff, northward, southward):
    slopes = pick_slope(limiter_code, back_diff, fore_diff)
    rising = northward * (values + 0.5 * (1.0 - northward) * slopes)
    sinking = southward * (values - 0.5 * (1.0 - southward) * slopes)
    return rising, sinking


def zonal_flux(fields, eastward, limiter):
    back_diff = fields - jnp.roll(fields, 1, axis=3)
    fore_diff = jnp.roll(fields, -1, axis=3) - fields
    slopes = pick_slope(limiter[None], back_diff, fore_diff)
    outgoing = eastward[None] * (fields + 0.5 * (1.0 - eastward[None]) * slopes)
    return outgoing, jnp.roll(outgoing, 1, axis=3)


def combine(fields, rising, sinking, from_below, from_above, outgoing, incoming):
    return fields - (rising + sinking) + (from_below + from_above) - (outgoing - incoming)


def regrid_column(layer_fields, layer_depth):
    levels = layer_depth.shape[0]
    top_edge = jnp.cumsum(layer_depth, axis=0)
    low_edge = top_edge - layer_depth
    target = top_edge[-1] / levels
    level_index = jnp.arange(levels, dtype=jnp.float32)[:, None]
    target_low = level_index * target[None]
    target_high = (level_index + 1.0) * target[None]
    intersection = jnp.maximum(jnp.minimum(top_edge[None], target_high[:, None]) - jnp.maximum(low_edge[None], target_low[:, None]), 0.0)
    shifted = jnp.einsum("kjc,fjc->fkc", intersection, layer_fields, precision=lax.Precision.HIGHEST)
    return shifted / target[None, None], target


def shortwave(packet, absorb, solar_flux):
    levels = (packet.shape[0] - 1) // 2
    vapour = packet[:levels]
    ozone_mix = packet[levels:2 * levels]
    layer_depth = packet[2 * levels]
    opacity = absorb[0][:, None, None] * (vapour * vapour)[None] + absorb[1][:, None, None] * (ozone_mix * ozone_mix)[None]
    optical = opacity * layer_depth[None, None]
    running = jnp.cumsum(optical, axis=1)
    overhead = jnp.concatenate([jnp.zeros_like(running[:, :1]), running[:, :-1]], 1)
    incoming = solar_flux[:, None, None] * jnp.exp(-overhead)
    absorbed = jnp.sum(incoming * (1.0 - jnp.exp(-optical)), axis=0)
    return absorbed / layer_depth[None]


def longwave(temper):
    beneath = jnp.concatenate([jnp.zeros_like(temper[:1]), temper[:-1]], 0)
    overlying = jnp.concatenate([temper[1:], jnp.zeros_like(temper[:1])], 0)
    return lw_rate * (beneath + overlying - 2.0 * temper) - lw_damp * temper


def reference(fields, north_courant, south_courant, east_courant, limiter, thickness, sunlit, absorb, solar_flux):
    padded = jnp.pad(fields, ((0, 0), (0, 0), (1, 1), (0, 0)))
    back_diff = fields - padded[:, :, :-2]
    fore_diff = padded[:, :, 2:] - fields
    rising, sinking = face_fluxes(fields, limiter[None], back_diff, fore_diff, north_courant[None], south_courant[None])
    zero_row = jnp.zeros_like(fields[:, :, :1])
    from_below = jnp.concatenate([zero_row, rising[:, :, :-1]], 2)
    from_above = jnp.concatenate([sinking[:, :, 1:], zero_row], 2)
    outgoing, incoming = zonal_flux(fields, east_courant, limiter)
    advected = combine(fields, rising, sinking, from_below, from_above, outgoing, incoming)
    lit_cols = jnp.repeat(sunlit.astype(jnp.float32), COLS_DEV, axis=1)

    def per_row(row_args):
        row_fields, row_depth, row_lit = row_args
        regridded, layer_depth = regrid_column(row_fields, row_depth)
        packet = jnp.concatenate([regridded[1], regridded[2], layer_depth[None]], 0)
        solar_heat = shortwave(packet, absorb, solar_flux)
        heating = solar_heat * row_lit[None] + longwave(regridded[0])
        return jnp.concatenate([(regridded[0] + heating)[None], regridded[1:]], 0)

    result = lax.map(per_row, (jnp.moveaxis(advected, 2, 0), jnp.moveaxis(thickness, 1, 0), lit_cols))
    return jnp.moveaxis(result, 0, 2)
```

```python
import math

import jax
import jax.numpy as jnp
from jax import lax
from jax.experimental import pallas as pl
from jax.experimental.pallas import tpu as pltpu
from jax.sharding import PartitionSpec as P

lw_rate = 0.2
lw_damp = 0.1
LANES = 128
least_thick = 0.5
most_thick = 2.0
kernel_vmem = 8 * 1024 * 1024


def passed_along(x, axis, by):
    size = lax.axis_size(axis)
    pairs = [(i, i + by) for i in range(size) if 0 <= i + by < size]
    return lax.ppermute(x, axis, pairs)


def block_rows(x):
    lead, (levels, rows, cols) = x.shape[:-3], x.shape[-3:]
    x = x.reshape(*lead, levels, rows, cols // LANES, LANES)
    return jnp.swapaxes(x, -3, -2).reshape(*lead, levels * rows * cols // LANES, LANES)


def row_of(ref, row, levels, blocks, lead=()):
    return jnp.concatenate(
        [ref[(*lead, pl.ds(2 * b + row, levels, stride=2 * blocks), slice(None))] for b in range(blocks)],
        axis=1,
    )


def slope_weights(code):
    wb = jnp.where(code == 1, 1.0, jnp.where(code == 3, 0.5, 0.0))
    wf = jnp.where(code == 2, 1.0, jnp.where(code == 3, 0.5, 0.0))
    return wb, wf


def pack_body(levels, blocks, fields, north, south, limiter, up, down):
    nc = row_of(north, 1, levels, blocks)
    wb, wf = slope_weights(row_of(limiter, 1, levels, blocks))
    gain = nc * (0.5 * (1.0 - nc))
    up[6] = gain * wf
    sc = row_of(south, 0, levels, blocks)
    vb, vf = slope_weights(row_of(limiter, 0, levels, blocks))
    loss = sc * (0.5 * (1.0 - sc))
    down[6] = loss * vb
    for f in range(3):
        low = row_of(fields, 0, levels, blocks, (f,))
        top = row_of(fields, 1, levels, blocks, (f,))
        step = top - low
        up[f] = top
        up[3 + f] = nc * top + gain * (wb * step - wf * top)
        down[f] = low
        down[3 + f] = sc * low - loss * (vb * low + vf * step)


def advect_body(levels, blocks, fields, north, south, east, limiter, thick, below, above, out):
    lane = lax.broadcasted_iota(jnp.int32, (levels, blocks * LANES), 1)
    cols = blocks * LANES
    weights, rise_gain, sink_gain, ncs, scs = [], [], [], [], []
    for r in range(2):
        weights.append(slope_weights(row_of(limiter, r, levels, blocks)))
        nc = row_of(north, r, levels, blocks)
        sc = row_of(south, r, levels, blocks)
        ncs.append(nc)
        scs.append(sc)
        rise_gain.append(nc * (0.5 * (1.0 - nc)))
        sink_gain.append(sc * (0.5 * (1.0 - sc)))
    ecs = [row_of(east, r, levels, blocks) for r in range(2)]
    east_gain = [ec * (0.5 * (1.0 - ec)) for ec in ecs]
    for f in range(3):
        rows = [row_of(fields, r, levels, blocks, (f,)) for r in range(2)]
        before = below[f]
        after = above[f]
        diffs = [rows[0] - before, rows[1] - rows[0], after - rows[1]]
        rise, sink, kept = [], [], []
        for r in range(2):
            wb, wf = weights[r]
            slope = wb * diffs[r] + wf * diffs[r + 1]
            rise.append(ncs[r] * rows[r] + rise_gain[r] * slope)
            sink.append(scs[r] * rows[r] - sink_gain[r] * slope)
            step = rows[r] - pltpu.roll(rows[r], 1, 1)
            zonal = wb * step + wf * pltpu.roll(step, cols - 1, 1)
            going = ecs[r] * rows[r] + east_gain[r] * zonal
            kept.append(rows[r] - (going - pltpu.roll(going, 1, 1)))
        from_below = below[3 + f] + below[6] * rows[0]
        from_above = above[3 + f] + above[6] * rows[1]
        first = kept[0] - (rise[0] + sink[0]) + (from_below + sink[1])
        second = kept[1] - (rise[1] + sink[1]) + (rise[0] + from_above)
        for r, value in enumerate((first, second)):
            for b in range(blocks):
                out[b, pl.ds((r * 4 + f) * levels, levels), :] = value[:, b * LANES : (b + 1) * LANES]
    for r in range(2):
        for b in range(blocks):
            out[b, pl.ds((r * 4 + 3) * levels, levels), :] = thick[pl.ds(2 * b + r, levels, stride=2 * blocks), :]


def reach(first, last, levels):
    ratio = most_thick / least_thick
    lo, hi = first / levels, last / levels
    low = levels * lo / (ratio - (ratio - 1.0) * lo)
    high = levels * ratio * hi / (1.0 + (ratio - 1.0) * hi)
    return max(0, math.floor(low) - 1), min(levels, math.ceil(high) + 1)


def column_body(sources, per, bands, got, lit, absorb, flux, out, thick_s, low_s, top_s, adv_s, pad_s):
    levels = sources * per
    cols = LANES
    for r in range(2):
        for s in range(sources):
            for f in range(3):
                adv_s[r, f, pl.ds(s * per, per), :] = got[s, pl.ds((r * 4 + f) * per, per), :]
            thick_s[r, pl.ds(s * per, per), :] = got[s, pl.ds((r * 4 + 3) * per, per), :]
    at_row = lax.broadcasted_iota(jnp.int32, (levels, levels), 0)
    at_col = lax.broadcasted_iota(jnp.int32, (levels, levels), 1)
    triangle = jnp.where(at_row >= at_col, 1.0, 0.0).astype(jnp.float32)

    def running(x):
        return jnp.dot(triangle, x, precision=lax.Precision.HIGHEST, preferred_element_type=jnp.float32)

    thick = jnp.concatenate([thick_s[0], thick_s[1]], axis=1)
    top = running(thick)
    low = top - thick
    step = 8
    depths, inverse = [], []
    for r in range(2):
        top_s[r] = top[:, r * cols : (r + 1) * cols]
        low_s[r] = low[:, r * cols : (r + 1) * cols]
        depth = top_s[r, pl.ds(levels - 1, 1), :] * (1.0 / levels)
        depths.append(depth)
        inverse.append(1.0 / depth)
    sub = lax.broadcasted_iota(jnp.int32, (step, cols), 0).astype(jnp.float32)
    squares = [[], []]
    for r in range(2):
        depth8 = jnp.broadcast_to(depths[r], (step, cols))
        inv8 = jnp.broadcast_to(inverse[r], (step, cols))
        for k in range(0, levels, step):
            start, stop = reach(k, k + step, levels)
            bottom = (sub + float(k)) * depth8
            ceiling = (sub + float(k + 1)) * depth8
            sums = [jnp.zeros((step, cols), jnp.float32)] * 3
            for j in range(start, stop):
                edge_top = jnp.broadcast_to(top_s[r, pl.ds(j, 1), :], (step, cols))
                edge_low = jnp.broadcast_to(low_s[r, pl.ds(j, 1), :], (step, cols))
                shared = jnp.maximum(jnp.minimum(edge_top, ceiling) - jnp.maximum(edge_low, bottom), 0.0)
                for f in range(3):
                    sums[f] = sums[f] + shared * jnp.broadcast_to(adv_s[r, f, pl.ds(j, 1), :], (step, cols))
            values = [total * inv8 for total in sums]
            pad_s[r, pl.ds(step + k, step), :] = values[0]
            out[1, pl.ds(2 * k + r, step, stride=2), :] = values[1]
            out[2, pl.ds(2 * k + r, step, stride=2), :] = values[2]
            squares[r].append((values[1] * values[1] * depth8, values[2] * values[2] * depth8))
    stacked = jnp.concatenate(
        [jnp.concatenate([s[i] for s in squares[r]], axis=0) for r in range(2) for i in range(2)], axis=1
    )
    path = running(stacked)
    log2e = 1.4426950408889634
    paths = [path[:, i * cols : (i + 1) * cols] for i in range(4)]

    def one_band(b, sums):
        a0 = absorb[0, b] * (-log2e)
        a1 = absorb[1, b] * (-log2e)
        power = flux[b]
        return tuple(
            sums[r] + power * jnp.exp2(a0 * paths[2 * r] + a1 * paths[2 * r + 1]) for r in range(2)
        )

    zero = jnp.zeros((levels, cols), jnp.float32)
    light = (zero, zero)
    for b in range(bands):
        light = one_band(b, light)
    full = flux[0]
    for b in range(1, bands):
        full = full + flux[b]
    for r in range(2):
        top_s[r] = light[r]
        for s in range(0, levels, step):
            if s == 0:
                upper = jnp.concatenate([jnp.full((1, cols), full, jnp.float32), light[r][: step - 1]], axis=0)
            else:
                upper = top_s[r, pl.ds(s - 1, step), :]
            pad_s[2 + r, pl.ds(s, step), :] = upper
        pad_s[r, pl.ds(0, step), :] = jnp.zeros((step, cols), jnp.float32)
        pad_s[r, pl.ds(step + levels, step), :] = jnp.zeros((step, cols), jnp.float32)
        absorbed = (pad_s[2 + r, pl.ds(0, levels), :] - light[r]) * inverse[r]
        heat = absorbed * lit[r].astype(jnp.float32)
        here = pad_s[r, pl.ds(step, levels), :]
        beneath = pad_s[r, pl.ds(step - 1, levels), :]
        overlying = pad_s[r, pl.ds(step + 1, levels), :]
        cooling = lw_rate * (beneath + overlying - 2.0 * here) - lw_damp * here
        out[0, pl.ds(r, levels, stride=2), :] = here + (heat + cooling)


def local(fields, north, south, east, limiter, thickness, sunlit, absorb, solar_flux):
    _, levels, _, cols = fields.shape
    blocks = cols // LANES
    sources = lax.axis_size("lev")
    vmem = pl.BlockSpec(memory_space=pltpu.VMEM)
    smem = pl.BlockSpec(memory_space=pltpu.SMEM)
    fields_v, north_v, south_v, east_v, limiter_v, thick_v = (
        block_rows(x) for x in (fields, north, south, east, limiter, thickness)
    )
    halo = jax.ShapeDtypeStruct((7, levels, cols), jnp.float32)
    up, down = pl.pallas_call(
        lambda *refs: pack_body(levels, blocks, *refs),
        out_shape=(halo, halo),
        in_specs=[vmem] * 4,
        out_specs=(vmem, vmem),
        compiler_params=pltpu.CompilerParams(vmem_limit_bytes=kernel_vmem),
        name="pack",
    )(fields_v, north_v, south_v, limiter_v)
    below = passed_along(up, "lat", 1)
    above = passed_along(down, "lat", -1)
    pieces = pl.pallas_call(
        lambda *refs: advect_body(levels, blocks, *refs),
        out_shape=jax.ShapeDtypeStruct((blocks, 8 * levels, LANES), jnp.float32),
        in_specs=[vmem] * 8,
        out_specs=vmem,
        compiler_params=pltpu.CompilerParams(vmem_limit_bytes=kernel_vmem),
        name="advect",
    )(fields_v, north_v, south_v, east_v, limiter_v, thick_v, below, above)
    got = lax.all_to_all(pieces, "lev", 0, 0)
    whole = sources * levels
    result = pl.pallas_call(
        lambda *refs: column_body(sources, levels, absorb.shape[1], *refs),
        out_shape=jax.ShapeDtypeStruct((3, whole * 2, LANES), jnp.float32),
        in_specs=[vmem, smem, smem, smem],
        out_specs=vmem,
        scratch_shapes=[
            pltpu.VMEM((2, whole, LANES), jnp.float32),
            pltpu.VMEM((2, whole, LANES), jnp.float32),
            pltpu.VMEM((2, whole, LANES), jnp.float32),
            pltpu.VMEM((2, 3, whole, LANES), jnp.float32),
            pltpu.VMEM((4, whole + 16, LANES), jnp.float32),
        ],
        compiler_params=pltpu.CompilerParams(vmem_limit_bytes=kernel_vmem),
        name="column",
    )(got, sunlit.reshape(-1), absorb, solar_flux)
    return result.reshape(3, whole, 2, LANES)


def solution(mesh):
    in_specs = (
        P(None, "lev", "lat", None),
        P("lev", "lat", None),
        P("lev", "lat", None),
        P("lev", "lat", None),
        P("lev", "lat", None),
        P("lev", "lat", None),
        P("lat", "lev"),
        P(),
        P(),
    )
    out_specs = P(None, None, "lat", "lev")
    return jax.shard_map(local, mesh=mesh, in_specs=in_specs, out_specs=out_specs, check_vma=False)
```

```python
import math

import jax
import jax.numpy as jnp
from jax import lax
from jax.experimental import pallas as pl
from jax.experimental.pallas import tpu as pltpu
from jax.sharding import PartitionSpec as P

lw_rate = 0.2
lw_damp = 0.1
LANES = 128
least_thick = 0.5
most_thick = 2.0
kernel_vmem = 8 * 1024 * 1024
log2e = 1.4426950408889634


def block_rows(x):
    lead, (levels, rows, cols) = x.shape[:-3], x.shape[-3:]
    x = x.reshape(*lead, levels, rows, cols // LANES, LANES)
    return jnp.swapaxes(x, -3, -2).reshape(*lead, levels * rows * cols // LANES, LANES)


def row_of(ref, row, levels, blocks, lead=()):
    return jnp.concatenate(
        [ref[(*lead, pl.ds(2 * b + row, levels, stride=2 * blocks), slice(None))] for b in range(blocks)],
        axis=1,
    )


def slope_weights(code):
    wb = jnp.where(code == 1, 1.0, jnp.where(code == 3, 0.5, 0.0))
    wf = jnp.where(code == 2, 1.0, jnp.where(code == 3, 0.5, 0.0))
    return wb, wf


def pack_body(levels, blocks, *refs):
    sources, near, far, held, sems = refs[:6], refs[6], refs[7], refs[8:14], refs[14]
    copies = [pltpu.make_async_copy(src, dst, sems.at[i]) for i, (src, dst) in enumerate(zip(sources, held))]
    for copy in copies:
        copy.start()
    for copy in copies[:4]:
        copy.wait()
    fields, north, south, limiter = held[:4]

    def pack(up, down):
        nc = row_of(north, 1, levels, blocks)
        wb, wf = slope_weights(row_of(limiter, 1, levels, blocks))
        gain = nc * (0.5 * (1.0 - nc))
        up[6] = gain * wf
        sc = row_of(south, 0, levels, blocks)
        vb, vf = slope_weights(row_of(limiter, 0, levels, blocks))
        loss = sc * (0.5 * (1.0 - sc))
        down[6] = loss * vb
        for f in range(3):
            low = row_of(fields, 0, levels, blocks, (f,))
            top = row_of(fields, 1, levels, blocks, (f,))
            step = top - low
            up[f] = top
            up[3 + f] = nc * top + gain * (wb * step - wf * top)
            down[f] = low
            down[3 + f] = sc * low - loss * (vb * low + vf * step)

    odd = lax.rem(lax.axis_index("lat"), 2) == 1
    pl.when(jnp.logical_not(odd))(lambda: pack(near, far))
    pl.when(odd)(lambda: pack(far, near))
    for copy in copies[4:]:
        copy.wait()


def prepare_body(bands, lit, absorb, flux, powers, daylight):
    for b in range(bands):
        powers[pl.ds(b, 1), :] = jnp.full((1, LANES), absorb[0, b] * (-log2e), jnp.float32)
        powers[pl.ds(bands + b, 1), :] = jnp.full((1, LANES), absorb[1, b] * (-log2e), jnp.float32)
        powers[pl.ds(2 * bands + b, 1), :] = jnp.full((1, LANES), flux[b], jnp.float32)
    for r in range(2):
        daylight[r] = jnp.full((8, LANES), lit[r].astype(jnp.float32), jnp.float32)


def advect_body(levels, blocks, *refs):
    near, far = refs[6:8]
    odd = lax.rem(lax.axis_index("lat"), 2) == 1
    pl.when(jnp.logical_not(odd))(lambda: advect(levels, blocks, *refs[:6], far, near, refs[10]))
    pl.when(odd)(lambda: advect(levels, blocks, *refs[:6], near, far, refs[10]))


def advect(levels, blocks, fields, north, south, limiter, east, thick, below, above, out):
    cols = blocks * LANES
    weights, rise_gain, sink_gain, ncs, scs = [], [], [], [], []
    for r in range(2):
        weights.append(slope_weights(row_of(limiter, r, levels, blocks)))
        nc = row_of(north, r, levels, blocks)
        sc = row_of(south, r, levels, blocks)
        ncs.append(nc)
        scs.append(sc)
        rise_gain.append(nc * (0.5 * (1.0 - nc)))
        sink_gain.append(sc * (0.5 * (1.0 - sc)))
    ecs = [row_of(east, r, levels, blocks) for r in range(2)]
    east_gain = [ec * (0.5 * (1.0 - ec)) for ec in ecs]
    for f in range(3):
        rows = [row_of(fields, r, levels, blocks, (f,)) for r in range(2)]
        before = below[f]
        after = above[f]
        diffs = [rows[0] - before, rows[1] - rows[0], after - rows[1]]
        rise, sink, kept = [], [], []
        for r in range(2):
            wb, wf = weights[r]
            slope = wb * diffs[r] + wf * diffs[r + 1]
            rise.append(ncs[r] * rows[r] + rise_gain[r] * slope)
            sink.append(scs[r] * rows[r] - sink_gain[r] * slope)
            step = rows[r] - pltpu.roll(rows[r], 1, 1)
            zonal = wb * step + wf * pltpu.roll(step, cols - 1, 1)
            going = ecs[r] * rows[r] + east_gain[r] * zonal
            kept.append(rows[r] - (going - pltpu.roll(going, 1, 1)))
        from_below = below[3 + f] + below[6] * rows[0]
        from_above = above[3 + f] + above[6] * rows[1]
        first = kept[0] - (rise[0] + sink[0]) + (from_below + sink[1])
        second = kept[1] - (rise[1] + sink[1]) + (rise[0] + from_above)
        for r, value in enumerate((first, second)):
            for b in range(blocks):
                out[b, pl.ds((r * 4 + f) * levels, levels), :] = value[:, b * LANES : (b + 1) * LANES]
    for r in range(2):
        for b in range(blocks):
            out[b, pl.ds((r * 4 + 3) * levels, levels), :] = thick[pl.ds(2 * b + r, levels, stride=2 * blocks), :]


def reach(first, last, levels):
    ratio = most_thick / least_thick
    lo, hi = first / levels, last / levels
    low = levels * lo / (ratio - (ratio - 1.0) * lo)
    high = levels * ratio * hi / (1.0 + (ratio - 1.0) * hi)
    return max(0, math.floor(low) - 1), min(levels, math.ceil(high) + 1)


def column_body(sources, per, bands, got, powers, daylight, out_h, thick_s, low_s, top_s, adv_s, pad_s, out, sems):
    levels = sources * per
    cols = LANES
    for r in range(2):
        for s in range(sources):
            for f in range(3):
                adv_s[r, f, pl.ds(s * per, per), :] = got[s, pl.ds((r * 4 + f) * per, per), :]
            thick_s[r, pl.ds(s * per, per), :] = got[s, pl.ds((r * 4 + 3) * per, per), :]
    at_row = lax.broadcasted_iota(jnp.int32, (levels, levels), 0)
    at_col = lax.broadcasted_iota(jnp.int32, (levels, levels), 1)
    triangle = jnp.where(at_row >= at_col, 1.0, 0.0).astype(jnp.float32)

    def running(x):
        return jnp.dot(triangle, x, precision=lax.Precision.HIGHEST, preferred_element_type=jnp.float32)

    thick = jnp.concatenate([thick_s[0], thick_s[1]], axis=1)
    top = running(thick)
    low = top - thick
    step = 8
    depths, inverse = [], []
    for r in range(2):
        top_s[r] = top[:, r * cols : (r + 1) * cols]
        low_s[r] = low[:, r * cols : (r + 1) * cols]
        depth = top_s[r, pl.ds(levels - 1, 1), :] * (1.0 / levels)
        depths.append(depth)
        inverse.append(1.0 / depth)
    sub = lax.broadcasted_iota(jnp.int32, (step, cols), 0).astype(jnp.float32)
    squares = [[], []]
    for r in range(2):
        depth8 = jnp.broadcast_to(depths[r], (step, cols))
        inv8 = jnp.broadcast_to(inverse[r], (step, cols))
        for k in range(0, levels, step):
            start, stop = reach(k, k + step, levels)
            bottom = (sub + float(k)) * depth8
            ceiling = (sub + float(k + 1)) * depth8
            sums = [jnp.zeros((step, cols), jnp.float32)] * 3
            for j in range(start, stop):
                edge_top = jnp.broadcast_to(top_s[r, pl.ds(j, 1), :], (step, cols))
                edge_low = jnp.broadcast_to(low_s[r, pl.ds(j, 1), :], (step, cols))
                shared = jnp.maximum(jnp.minimum(edge_top, ceiling) - jnp.maximum(edge_low, bottom), 0.0)
                for f in range(3):
                    sums[f] = sums[f] + shared * jnp.broadcast_to(adv_s[r, f, pl.ds(j, 1), :], (step, cols))
            values = [total * inv8 for total in sums]
            pad_s[r, pl.ds(step + k, step), :] = values[0]
            out[1, pl.ds(2 * k + r, step, stride=2), :] = values[1]
            out[2, pl.ds(2 * k + r, step, stride=2), :] = values[2]
            squares[r].append((values[1] * values[1] * depth8, values[2] * values[2] * depth8))
    copies = [pltpu.make_async_copy(out.at[f], out_h.at[f], sems.at[f]) for f in range(3)]
    copies[1].start()
    copies[2].start()
    stacked = jnp.concatenate(
        [jnp.concatenate([s[i] for s in squares[r]], axis=0) for r in range(2) for i in range(2)], axis=1
    )
    path = running(stacked)
    paths = [path[:, i * cols : (i + 1) * cols] for i in range(4)]
    light = [jnp.zeros((levels, cols), jnp.float32)] * 2
    full = jnp.zeros((1, cols), jnp.float32)
    for b in range(bands):
        a0 = jnp.broadcast_to(powers[pl.ds(b, 1), :], (levels, cols))
        a1 = jnp.broadcast_to(powers[pl.ds(bands + b, 1), :], (levels, cols))
        power = jnp.broadcast_to(powers[pl.ds(2 * bands + b, 1), :], (levels, cols))
        full = full + powers[pl.ds(2 * bands + b, 1), :]
        for r in range(2):
            light[r] = light[r] + power * jnp.exp2(a0 * paths[2 * r] + a1 * paths[2 * r + 1])
    for r in range(2):
        top_s[r] = light[r]
        upper = [jnp.concatenate([full, light[r][: step - 1]], axis=0)]
        upper += [top_s[r, pl.ds(s - 1, step), :] for s in range(step, levels, step)]
        absorbed = (jnp.concatenate(upper, axis=0) - light[r]) * inverse[r]
        heat = absorbed * daylight[r, pl.ds(0, 1), :]
        pad_s[r, pl.ds(0, step), :] = jnp.zeros((step, cols), jnp.float32)
        pad_s[r, pl.ds(step + levels, step), :] = jnp.zeros((step, cols), jnp.float32)
        here = pad_s[r, pl.ds(step, levels), :]
        beneath = pad_s[r, pl.ds(step - 1, levels), :]
        overlying = pad_s[r, pl.ds(step + 1, levels), :]
        cooling = lw_rate * (beneath + overlying - 2.0 * here) - lw_damp * here
        out[0, pl.ds(r, levels, stride=2), :] = here + (heat + cooling)
    copies[0].start()
    for copy in copies:
        copy.wait()


def swapped(x, axis, first):
    size = lax.axis_size(axis)
    pairs = [(i, i + 1) for i in range(first, size - 1, 2)]
    return lax.ppermute(x, axis, [way for i, j in pairs for way in ((i, j), (j, i))])


def local(fields, north, south, east, limiter, thickness, sunlit, absorb, solar_flux):
    _, levels, _, cols = fields.shape
    blocks = cols // LANES
    bands = absorb.shape[1]
    sources = lax.axis_size("lev")
    vmem = pl.BlockSpec(memory_space=pltpu.VMEM)
    smem = pl.BlockSpec(memory_space=pltpu.SMEM)
    hbm = pl.BlockSpec(memory_space=pltpu.HBM)
    params = pltpu.CompilerParams(vmem_limit_bytes=kernel_vmem)
    given = [pltpu.with_memory_space_constraint(block_rows(x), pltpu.HBM) for x in (fields, north, south, limiter, east, thickness)]
    halo = jax.ShapeDtypeStruct((7, levels, cols), jnp.float32)
    near, far, *held = pl.pallas_call(
        lambda *refs: pack_body(levels, blocks, *refs),
        out_shape=[halo, halo] + [jax.ShapeDtypeStruct(x.shape, x.dtype) for x in given],
        in_specs=[hbm] * 6,
        out_specs=[vmem] * 8,
        scratch_shapes=[pltpu.SemaphoreType.DMA((6,))],
        compiler_params=params,
        name="pack",
    )(*given)
    far = swapped(far, "lat", 1)
    near = swapped(near, "lat", 0)
    powers, daylight = pl.pallas_call(
        lambda *refs: prepare_body(bands, *refs),
        out_shape=(jax.ShapeDtypeStruct((3 * bands, LANES), jnp.float32), jax.ShapeDtypeStruct((2, 8, LANES), jnp.float32)),
        in_specs=[smem] * 3,
        out_specs=(vmem, vmem),
        compiler_params=params,
        cost_estimate=pl.CostEstimate(flops=100000, bytes_accessed=1000000, transcendentals=0),
        name="prepare",
    )(sunlit.reshape(-1), absorb, solar_flux)
    pieces = pl.pallas_call(
        lambda *refs: advect_body(levels, blocks, *refs),
        out_shape=jax.ShapeDtypeStruct((blocks, 8 * levels, LANES), jnp.float32),
        in_specs=[vmem] * 10,
        out_specs=vmem,
        compiler_params=params,
        name="advect",
    )(*held, near, far, powers, daylight)
    got = lax.all_to_all(pieces, "lev", 0, 0)
    whole = sources * levels
    result = pl.pallas_call(
        lambda *refs: column_body(sources, levels, bands, *refs),
        out_shape=jax.ShapeDtypeStruct((3, whole * 2, LANES), jnp.float32),
        in_specs=[vmem] * 3,
        out_specs=hbm,
        scratch_shapes=[
            pltpu.VMEM((2, whole, LANES), jnp.float32),
            pltpu.VMEM((2, whole, LANES), jnp.float32),
            pltpu.VMEM((2, whole, LANES), jnp.float32),
            pltpu.VMEM((2, 3, whole, LANES), jnp.float32),
            pltpu.VMEM((2, whole + 16, LANES), jnp.float32),
            pltpu.VMEM((3, whole * 2, LANES), jnp.float32),
            pltpu.SemaphoreType.DMA((3,)),
        ],
        compiler_params=params,
        name="column",
    )(got, powers, daylight)
    return result.reshape(3, whole, 2, LANES)


def solution(mesh):
    in_specs = (
        P(None, "lev", "lat", None),
        P("lev", "lat", None),
        P("lev", "lat", None),
        P("lev", "lat", None),
        P("lev", "lat", None),
        P("lev", "lat", None),
        P("lat", "lev"),
        P(),
        P(),
    )
    out_specs = P(None, None, "lat", "lev")
    return jax.shard_map(local, mesh=mesh, in_specs=in_specs, out_specs=out_specs, check_vma=False)
```

```python
import math

import jax
import jax.numpy as jnp
from jax import lax
from jax.experimental import pallas as pl
from jax.experimental.pallas import tpu as pltpu
from jax.sharding import PartitionSpec as P


lw_rate = 0.2
lw_damp = 0.1
LANES = 128
least_thick = 0.5
most_thick = 2.0
kernel_vmem = 8 * 1024 * 1024
log2e = 1.4426950408889634


def block_rows(x):
    lead, (levels, rows, cols) = x.shape[:-3], x.shape[-3:]
    x = x.reshape(*lead, levels, rows, cols // LANES, LANES)
    return jnp.swapaxes(x, -3, -2).reshape(*lead, levels * rows * cols // LANES, LANES)


def row_of(ref, row, levels, blocks, lead=()):
    return jnp.concatenate(
        [ref[(*lead, pl.ds(2 * b + row, levels, stride=2 * blocks), slice(None))] for b in range(blocks)],
        axis=1,
    )


def slope_weights(code):
    wb = jnp.where(code == 1, 1.0, jnp.where(code == 3, 0.5, 0.0))
    wf = jnp.where(code == 2, 1.0, jnp.where(code == 3, 0.5, 0.0))
    return wb, wf


def pack_body(levels, blocks, *refs):
    sources, near, far, held, sems = refs[:6], refs[6], refs[7], refs[8:14], refs[14]
    copies = [pltpu.make_async_copy(src, dst, sems.at[i]) for i, (src, dst) in enumerate(zip(sources, held))]
    for copy in copies:
        copy.start()
    for copy in copies[:4]:
        copy.wait()
    fields, north, south, limiter = held[:4]

    def pack(up, down):
        nc = row_of(north, 1, levels, blocks)
        wb, wf = slope_weights(row_of(limiter, 1, levels, blocks))
        gain = nc * (0.5 * (1.0 - nc))
        up[6] = gain * wf
        sc = row_of(south, 0, levels, blocks)
        vb, vf = slope_weights(row_of(limiter, 0, levels, blocks))
        loss = sc * (0.5 * (1.0 - sc))
        down[6] = loss * vb
        for f in range(3):
            low = row_of(fields, 0, levels, blocks, (f,))
            top = row_of(fields, 1, levels, blocks, (f,))
            step = top - low
            up[f] = top
            up[3 + f] = nc * top + gain * (wb * step - wf * top)
            down[f] = low
            down[3 + f] = sc * low - loss * (vb * low + vf * step)

    odd = lax.rem(lax.axis_index("lat"), 2) == 1
    pl.when(jnp.logical_not(odd))(lambda: pack(near, far))
    pl.when(odd)(lambda: pack(far, near))
    for copy in copies[4:]:
        copy.wait()


def prepare_body(bands, lit, absorb, flux, powers, daylight):
    for b in range(bands):
        powers[pl.ds(b, 1), :] = jnp.full((1, LANES), absorb[0, b] * (-log2e), jnp.float32)
        powers[pl.ds(bands + b, 1), :] = jnp.full((1, LANES), absorb[1, b] * (-log2e), jnp.float32)
        powers[pl.ds(2 * bands + b, 1), :] = jnp.full((1, LANES), flux[b], jnp.float32)
    for r in range(2):
        daylight[r] = jnp.full((8, LANES), lit[r].astype(jnp.float32), jnp.float32)


def advect_body(levels, blocks, *refs):
    core = lax.rem(lax.axis_index("lev"), 2)
    pl.when(core == 0)(lambda: advect(levels, blocks, *refs[:8], refs[10], refs[11]))
    pl.when(core == 1)(lambda: advect(levels, blocks, *refs[:8], refs[11], refs[10]))


def advect(levels, blocks, fields, north, south, limiter, east, thick, near, far, even, odd):
    above_far = lax.rem(lax.axis_index("lat"), 2) == 1

    def below(i):
        return jnp.where(above_far, near[i], far[i])

    def above(i):
        return jnp.where(above_far, far[i], near[i])

    cols = blocks * LANES
    weights, rise_gain, sink_gain, ncs, scs = [], [], [], [], []
    for r in range(2):
        weights.append(slope_weights(row_of(limiter, r, levels, blocks)))
        nc = row_of(north, r, levels, blocks)
        sc = row_of(south, r, levels, blocks)
        ncs.append(nc)
        scs.append(sc)
        rise_gain.append(nc * (0.5 * (1.0 - nc)))
        sink_gain.append(sc * (0.5 * (1.0 - sc)))
    ecs = [row_of(east, r, levels, blocks) for r in range(2)]
    east_gain = [ec * (0.5 * (1.0 - ec)) for ec in ecs]
    for f in range(3):
        rows = [row_of(fields, r, levels, blocks, (f,)) for r in range(2)]
        before = below(f)
        after = above(f)
        diffs = [rows[0] - before, rows[1] - rows[0], after - rows[1]]
        rise, sink, kept = [], [], []
        for r in range(2):
            wb, wf = weights[r]
            slope = wb * diffs[r] + wf * diffs[r + 1]
            rise.append(ncs[r] * rows[r] + rise_gain[r] * slope)
            sink.append(scs[r] * rows[r] - sink_gain[r] * slope)
            step = rows[r] - pltpu.roll(rows[r], 1, 1)
            zonal = wb * step + wf * pltpu.roll(step, cols - 1, 1)
            going = ecs[r] * rows[r] + east_gain[r] * zonal
            kept.append(rows[r] - (going - pltpu.roll(going, 1, 1)))
        from_below = below(3 + f) + below(6) * rows[0]
        from_above = above(3 + f) + above(6) * rows[1]
        first = kept[0] - (rise[0] + sink[0]) + (from_below + sink[1])
        second = kept[1] - (rise[1] + sink[1]) + (rise[0] + from_above)
        for r, value in enumerate((first, second)):
            for b in range(blocks):
                out = (even, odd)[b % 2]
                out[b // 2, pl.ds((r * 4 + f) * levels, levels), :] = value[:, b * LANES : (b + 1) * LANES]
    for r in range(2):
        for b in range(blocks):
            out = (even, odd)[b % 2]
            out[b // 2, pl.ds((r * 4 + 3) * levels, levels), :] = thick[pl.ds(2 * b + r, levels, stride=2 * blocks), :]


def join_body(kept, swapped_in, *out):
    place = lax.axis_index("lev")
    chip, core = lax.shift_right_logical(place, 1), lax.rem(place, 2)
    for q in range(4):
        target = lax.bitwise_xor(chip, q)
        out[q][core] = kept[target]
        out[q][1 - core] = swapped_in[target]


def reach(first, last, levels):
    ratio = most_thick / least_thick
    lo, hi = first / levels, last / levels
    low = levels * lo / (ratio - (ratio - 1.0) * lo)
    high = levels * ratio * hi / (1.0 + (ratio - 1.0) * hi)
    return max(0, math.floor(low) - 1), min(levels, math.ceil(high) + 1)


def column_body(sources, per, bands, own, beside, low2, high2, low3, high3, powers, daylight, out_h, got, thick_s, low_s, top_s, adv_s, pad_s, out, sems):
    levels = sources * per
    cols = LANES
    chip = lax.shift_right_logical(lax.axis_index("lev"), 1)

    def place(pieces):
        for q, piece in enumerate(pieces):
            source = lax.bitwise_xor(chip, q)
            for c in range(2):
                got[2 * source + c] = piece[c]

    pl.when(chip < 2)(lambda: place((own, beside, low2, low3)))
    pl.when(chip >= 2)(lambda: place((own, beside, high2, high3)))
    for r in range(2):
        for s in range(sources):
            for f in range(3):
                adv_s[r, f, pl.ds(s * per, per), :] = got[s, pl.ds((r * 4 + f) * per, per), :]
            thick_s[r, pl.ds(s * per, per), :] = got[s, pl.ds((r * 4 + 3) * per, per), :]
    at_row = lax.broadcasted_iota(jnp.int32, (levels, levels), 0)
    at_col = lax.broadcasted_iota(jnp.int32, (levels, levels), 1)
    triangle = jnp.where(at_row >= at_col, 1.0, 0.0).astype(jnp.float32)

    def running(x):
        return jnp.dot(triangle, x, precision=lax.Precision.HIGHEST, preferred_element_type=jnp.float32)

    thick = jnp.concatenate([thick_s[0], thick_s[1]], axis=1)
    top = running(thick)
    low = top - thick
    step = 8
    depths, inverse = [], []
    for r in range(2):
        top_s[r] = top[:, r * cols : (r + 1) * cols]
        low_s[r] = low[:, r * cols : (r + 1) * cols]
        depth = top_s[r, pl.ds(levels - 1, 1), :] * (1.0 / levels)
        depths.append(depth)
        inverse.append(1.0 / depth)
    sub = lax.broadcasted_iota(jnp.int32, (step, cols), 0).astype(jnp.float32)
    squares = [[], []]
    for r in range(2):
        depth8 = jnp.broadcast_to(depths[r], (step, cols))
        inv8 = jnp.broadcast_to(inverse[r], (step, cols))
        for k in range(0, levels, step):
            start, stop = reach(k, k + step, levels)
            bottom = (sub + float(k)) * depth8
            ceiling = (sub + float(k + 1)) * depth8
            sums = [jnp.zeros((step, cols), jnp.float32)] * 3
            for j in range(start, stop):
                edge_top = jnp.broadcast_to(top_s[r, pl.ds(j, 1), :], (step, cols))
                edge_low = jnp.broadcast_to(low_s[r, pl.ds(j, 1), :], (step, cols))
                shared = jnp.maximum(jnp.minimum(edge_top, ceiling) - jnp.maximum(edge_low, bottom), 0.0)
                for f in range(3):
                    sums[f] = sums[f] + shared * jnp.broadcast_to(adv_s[r, f, pl.ds(j, 1), :], (step, cols))
            values = [total * inv8 for total in sums]
            pad_s[r, pl.ds(step + k, step), :] = values[0]
            out[1, pl.ds(2 * k + r, step, stride=2), :] = values[1]
            out[2, pl.ds(2 * k + r, step, stride=2), :] = values[2]
            squares[r].append((values[1] * values[1] * depth8, values[2] * values[2] * depth8))
    copies = [pltpu.make_async_copy(out.at[f], out_h.at[f], sems.at[f]) for f in range(3)]
    copies[1].start()
    copies[2].start()
    stacked = jnp.concatenate(
        [jnp.concatenate([s[i] for s in squares[r]], axis=0) for r in range(2) for i in range(2)], axis=1
    )
    path = running(stacked)
    paths = [path[:, i * cols : (i + 1) * cols] for i in range(4)]
    light = [jnp.zeros((levels, cols), jnp.float32)] * 2
    full = jnp.zeros((1, cols), jnp.float32)
    for b in range(bands):
        a0 = jnp.broadcast_to(powers[pl.ds(b, 1), :], (levels, cols))
        a1 = jnp.broadcast_to(powers[pl.ds(bands + b, 1), :], (levels, cols))
        power = jnp.broadcast_to(powers[pl.ds(2 * bands + b, 1), :], (levels, cols))
        full = full + powers[pl.ds(2 * bands + b, 1), :]
        for r in range(2):
            light[r] = light[r] + power * jnp.exp2(a0 * paths[2 * r] + a1 * paths[2 * r + 1])
    for r in range(2):
        top_s[r] = light[r]
        upper = [jnp.concatenate([full, light[r][: step - 1]], axis=0)]
        upper += [top_s[r, pl.ds(s - 1, step), :] for s in range(step, levels, step)]
        absorbed = (jnp.concatenate(upper, axis=0) - light[r]) * inverse[r]
        heat = absorbed * daylight[r, pl.ds(0, 1), :]
        pad_s[r, pl.ds(0, step), :] = jnp.zeros((step, cols), jnp.float32)
        pad_s[r, pl.ds(step + levels, step), :] = jnp.zeros((step, cols), jnp.float32)
        here = pad_s[r, pl.ds(step, levels), :]
        beneath = pad_s[r, pl.ds(step - 1, levels), :]
        overlying = pad_s[r, pl.ds(step + 1, levels), :]
        cooling = lw_rate * (beneath + overlying - 2.0 * here) - lw_damp * here
        out[0, pl.ds(r, levels, stride=2), :] = here + (heat + cooling)
    copies[0].start()
    for copy in copies:
        copy.wait()


def swapped(x, axis, first):
    size = lax.axis_size(axis)
    pairs = [(i, i + 1) for i in range(first, size - 1, 2)]
    return lax.ppermute(x, axis, [way for i, j in pairs for way in ((i, j), (j, i))])


def core_swap(x):
    size = lax.axis_size("lev")
    return lax.ppermute(x, "lev", [(i, i ^ 1) for i in range(size)])


def between_chips(x, pairs):
    return lax.ppermute(x, "lev", [(2 * a + c, 2 * b + c) for a, b in pairs for c in range(2)])


def local(fields, north, south, east, limiter, thickness, sunlit, absorb, solar_flux):
    _, levels, _, cols = fields.shape
    blocks = cols // LANES
    bands = absorb.shape[1]
    sources = lax.axis_size("lev")
    vmem = pl.BlockSpec(memory_space=pltpu.VMEM)
    smem = pl.BlockSpec(memory_space=pltpu.SMEM)
    hbm = pl.BlockSpec(memory_space=pltpu.HBM)
    params = pltpu.CompilerParams(vmem_limit_bytes=kernel_vmem)
    given = [pltpu.with_memory_space_constraint(block_rows(x), pltpu.HBM) for x in (fields, north, south, limiter, east, thickness)]
    halo = jax.ShapeDtypeStruct((7, levels, cols), jnp.float32)
    near, far, *held = pl.pallas_call(
        lambda *refs: pack_body(levels, blocks, *refs),
        out_shape=[halo, halo] + [jax.ShapeDtypeStruct(x.shape, x.dtype) for x in given],
        in_specs=[hbm] * 6,
        out_specs=[vmem] * 8,
        scratch_shapes=[pltpu.SemaphoreType.DMA((6,))],
        compiler_params=params,
        name="pack",
    )(*given)
    far = swapped(far, "lat", 1)
    near = swapped(near, "lat", 0)
    powers, daylight = pl.pallas_call(
        lambda *refs: prepare_body(bands, *refs),
        out_shape=(jax.ShapeDtypeStruct((3 * bands, LANES), jnp.float32), jax.ShapeDtypeStruct((2, 8, LANES), jnp.float32)),
        in_specs=[smem] * 3,
        out_specs=(vmem, vmem),
        compiler_params=params,
        cost_estimate=pl.CostEstimate(flops=100000, bytes_accessed=1000000, transcendentals=0),
        name="prepare",
    )(sunlit.reshape(-1), absorb, solar_flux)
    half = jax.ShapeDtypeStruct((sources // 2, 8 * levels, LANES), jnp.float32)
    kept, given_away = pl.pallas_call(
        lambda *refs: advect_body(levels, blocks, *refs),
        out_shape=(half, half),
        in_specs=[vmem] * 10,
        out_specs=(vmem, vmem),
        compiler_params=params,
        name="advect",
    )(*held, near, far, powers, daylight)
    pair = jax.ShapeDtypeStruct((2, 8 * levels, LANES), jnp.float32)
    own, beside, second, third = pl.pallas_call(
        join_body,
        out_shape=[pair] * 4,
        in_specs=[vmem] * 2,
        out_specs=[vmem] * 4,
        compiler_params=params,
        name="join",
    )(kept, core_swap(given_away))
    beside = between_chips(beside, ((0, 1), (1, 0), (2, 3), (3, 2)))
    low3 = between_chips(third, ((2, 1), (3, 0)))
    low2 = between_chips(second, ((2, 0), (3, 1)))
    high3 = between_chips(third, ((0, 3), (1, 2)))
    high2 = between_chips(second, ((0, 2), (1, 3)))
    whole = sources * levels
    result = pl.pallas_call(
        lambda *refs: column_body(sources, levels, bands, *refs),
        out_shape=jax.ShapeDtypeStruct((3, whole * 2, LANES), jnp.float32),
        in_specs=[vmem] * 8,
        out_specs=hbm,
        scratch_shapes=[
            pltpu.VMEM((sources, 8 * levels, LANES), jnp.float32),
            pltpu.VMEM((2, whole, LANES), jnp.float32),
            pltpu.VMEM((2, whole, LANES), jnp.float32),
            pltpu.VMEM((2, whole, LANES), jnp.float32),
            pltpu.VMEM((2, 3, whole, LANES), jnp.float32),
            pltpu.VMEM((2, whole + 16, LANES), jnp.float32),
            pltpu.VMEM((3, whole * 2, LANES), jnp.float32),
            pltpu.SemaphoreType.DMA((3,)),
        ],
        compiler_params=params,
        name="column",
    )(own, beside, low2, high2, low3, high3, powers, daylight)
    return result.reshape(3, whole, 2, LANES)


def solution(mesh):
    in_specs = (
        P(None, "lev", "lat", None),
        P("lev", "lat", None),
        P("lev", "lat", None),
        P("lev", "lat", None),
        P("lev", "lat", None),
        P("lev", "lat", None),
        P("lat", "lev"),
        P(),
        P(),
    )
    out_specs = P(None, None, "lat", "lev")

    return jax.shard_map(local, mesh=mesh, in_specs=in_specs, out_specs=out_specs, check_vma=False)
```

```python
import math

import jax
import jax.numpy as jnp
from jax import lax
from jax.experimental import pallas as pl
from jax.experimental.pallas import tpu as pltpu
from jax.sharding import PartitionSpec as P


lw_rate = 0.2
lw_damp = 0.1
LANES = 128
least_thick = 0.5
most_thick = 2.0
kernel_vmem = 8 * 1024 * 1024
log2e = 1.4426950408889634


def block_rows(x):
    lead, (levels, rows, cols) = x.shape[:-3], x.shape[-3:]
    x = x.reshape(*lead, levels, rows, cols // LANES, LANES)
    return jnp.swapaxes(x, -3, -2).reshape(*lead, levels * rows * cols // LANES, LANES)


def row_of(ref, row, levels, blocks, lead=()):
    return jnp.concatenate(
        [ref[(*lead, pl.ds(2 * b + row, levels, stride=2 * blocks), slice(None))] for b in range(blocks)],
        axis=1,
    )


def slope_weights(code):
    wb = jnp.where(code == 1, 1.0, jnp.where(code == 3, 0.5, 0.0))
    wf = jnp.where(code == 2, 1.0, jnp.where(code == 3, 0.5, 0.0))
    return wb, wf


def pack_body(levels, blocks, *refs):
    sources, near, far, held, sems = refs[:6], refs[6:8], refs[8:10], refs[10:16], refs[16]
    half = blocks * LANES // 2
    copies = [pltpu.make_async_copy(src, dst, sems.at[i]) for i, (src, dst) in enumerate(zip(sources, held))]
    for copy in copies:
        copy.start()
    for copy in copies[:4]:
        copy.wait()
    fields, north, south, limiter = held[:4]

    def put(halves, at, value):
        halves[0][at] = value[:, :half]
        halves[1][at] = value[:, half:]

    def pack(up, down):
        nc = row_of(north, 1, levels, blocks)
        wb, wf = slope_weights(row_of(limiter, 1, levels, blocks))
        gain = nc * (0.5 * (1.0 - nc))
        put(up, 6, gain * wf)
        sc = row_of(south, 0, levels, blocks)
        vb, vf = slope_weights(row_of(limiter, 0, levels, blocks))
        loss = sc * (0.5 * (1.0 - sc))
        put(down, 6, loss * vb)
        for f in range(3):
            low = row_of(fields, 0, levels, blocks, (f,))
            top = row_of(fields, 1, levels, blocks, (f,))
            step = top - low
            put(up, f, top)
            put(up, 3 + f, nc * top + gain * (wb * step - wf * top))
            put(down, f, low)
            put(down, 3 + f, sc * low - loss * (vb * low + vf * step))

    odd = lax.rem(lax.axis_index("lat"), 2) == 1
    pl.when(jnp.logical_not(odd))(lambda: pack(near, far))
    pl.when(odd)(lambda: pack(far, near))
    for copy in copies[4:]:
        copy.wait()


def prepare_body(bands, lit, absorb, flux, powers, daylight):
    for b in range(bands):
        powers[pl.ds(b, 1), :] = jnp.full((1, LANES), absorb[0, b] * (-log2e), jnp.float32)
        powers[pl.ds(bands + b, 1), :] = jnp.full((1, LANES), absorb[1, b] * (-log2e), jnp.float32)
        powers[pl.ds(2 * bands + b, 1), :] = jnp.full((1, LANES), flux[b], jnp.float32)
    for r in range(2):
        daylight[r] = jnp.full((8, LANES), lit[r].astype(jnp.float32), jnp.float32)


def advect_body(levels, blocks, part, *refs):
    core = lax.rem(lax.axis_index("lev"), 2)
    pl.when(core == 0)(lambda: advect(levels, blocks, part, *refs[:8], refs[-2], refs[-1]))
    pl.when(core == 1)(lambda: advect(levels, blocks, part, *refs[:8], refs[-1], refs[-2]))


def advect(levels, blocks, part, fields, north, south, limiter, east, thick, near, far, even, odd):
    above_far = lax.rem(lax.axis_index("lat"), 2) == 1
    cols = blocks * LANES
    first_block = part * (blocks // 2)

    def below(i):
        return jnp.where(above_far, near[i], far[i])

    def above(i):
        return jnp.where(above_far, far[i], near[i])

    def cut(value):
        return value[:, part * (cols // 2) : (part + 1) * (cols // 2)]

    weights, ncs, scs, ecs = [], [], [], []
    for r in range(2):
        weights.append(slope_weights(row_of(limiter, r, levels, blocks)))
        ncs.append(cut(row_of(north, r, levels, blocks)))
        scs.append(cut(row_of(south, r, levels, blocks)))
        ecs.append(row_of(east, r, levels, blocks))
    rise_gain = [nc * (0.5 * (1.0 - nc)) for nc in ncs]
    sink_gain = [sc * (0.5 * (1.0 - sc)) for sc in scs]
    east_gain = [ec * (0.5 * (1.0 - ec)) for ec in ecs]
    for f in range(3):
        whole = [row_of(fields, r, levels, blocks, (f,)) for r in range(2)]
        rows = [cut(row) for row in whole]
        diffs = [rows[0] - below(f), rows[1] - rows[0], above(f) - rows[1]]
        rise, sink, kept = [], [], []
        for r in range(2):
            wb, wf = weights[r]
            slope = cut(wb) * diffs[r] + cut(wf) * diffs[r + 1]
            rise.append(ncs[r] * rows[r] + rise_gain[r] * slope)
            sink.append(scs[r] * rows[r] - sink_gain[r] * slope)
            step = whole[r] - pltpu.roll(whole[r], 1, 1)
            zonal = wb * step + wf * pltpu.roll(step, cols - 1, 1)
            going = ecs[r] * whole[r] + east_gain[r] * zonal
            kept.append(rows[r] - cut(going - pltpu.roll(going, 1, 1)))
        from_below = below(3 + f) + below(6) * rows[0]
        from_above = above(3 + f) + above(6) * rows[1]
        first = kept[0] - (rise[0] + sink[0]) + (from_below + sink[1])
        second = kept[1] - (rise[1] + sink[1]) + (rise[0] + from_above)
        for r, value in enumerate((first, second)):
            for b in range(blocks // 2):
                (even, odd)[b % 2][b // 2, pl.ds((r * 4 + f) * levels, levels), :] = value[:, b * LANES : (b + 1) * LANES]
    for r in range(2):
        for b in range(blocks // 2):
            (even, odd)[b % 2][b // 2, pl.ds((r * 4 + 3) * levels, levels), :] = thick[
                pl.ds(2 * (first_block + b) + r, levels, stride=2 * blocks), :
            ]


def join_body(kept, swapped_in, across, straight):
    place = lax.axis_index("lev")
    core, parity = lax.rem(place, 2), lax.rem(lax.shift_right_logical(place, 1), 2)
    for out, target in ((across, 1 - parity), (straight, parity)):
        out[core] = kept[target]
        out[1 - core] = swapped_in[target]


def reach(first, last, levels):
    ratio = most_thick / least_thick
    lo, hi = first / levels, last / levels
    low = levels * lo / (ratio - (ratio - 1.0) * lo)
    high = levels * ratio * hi / (1.0 + (ratio - 1.0) * hi)
    return max(0, math.floor(low) - 1), min(levels, math.ceil(high) + 1)


def column_body(sources, per, bands, own1, beside1, second1, third1, own2, beside2, second2, third2, powers, daylight, out_h, got, low_s, top_s, pad_s, out, sems):
    levels = sources * per
    cols = LANES
    chip = lax.shift_right_logical(lax.axis_index("lev"), 1)

    def place(pieces):
        for q, piece in enumerate(pieces):
            source = lax.bitwise_xor(chip, q)
            for c in range(2):
                got[2 * source + c] = piece[c]

    pl.when(chip < 2)(lambda: place((own1, beside1, second1, third1)))
    pl.when(chip >= 2)(lambda: place((own2, beside2, second2, third2)))
    at_row = lax.broadcasted_iota(jnp.int32, (levels, levels), 0)
    at_col = lax.broadcasted_iota(jnp.int32, (levels, levels), 1)
    triangle = jnp.where(at_row >= at_col, 1.0, 0.0).astype(jnp.bfloat16)

    def running(x):
        total = None
        for _ in range(3):
            part = x.astype(jnp.bfloat16)
            x = x - part.astype(jnp.float32)
            sums = jnp.dot(triangle, part, preferred_element_type=jnp.float32)
            total = sums if total is None else total + sums
        return total

    def piece(s, r, f):
        return got[s, pl.ds((r * 4 + f) * per, per), :]

    def level(j, r, f):
        line = got[j // per, pl.ds((r * 4 + f) * per + j % per, 1), :]
        return jnp.broadcast_to(line, (8, cols))

    thick = jnp.concatenate(
        [jnp.concatenate([piece(s, r, 3) for s in range(sources)], axis=0) for r in range(2)], axis=1
    )
    top = running(thick)
    low = top - thick
    step = 8
    depths, inverse = [], []
    for r in range(2):
        top_s[r] = top[:, r * cols : (r + 1) * cols]
        low_s[r] = low[:, r * cols : (r + 1) * cols]
        depth = top_s[r, pl.ds(levels - 1, 1), :] * (1.0 / levels)
        depths.append(depth)
        inverse.append(1.0 / depth)
    sub = lax.broadcasted_iota(jnp.int32, (step, cols), 0).astype(jnp.float32)
    squares = [[], []]
    for r in range(2):
        depth8 = jnp.broadcast_to(depths[r], (step, cols))
        inv8 = jnp.broadcast_to(inverse[r], (step, cols))
        for k in range(0, levels, step):
            start, stop = reach(k, k + step, levels)
            bottom = (sub + float(k)) * depth8
            ceiling = (sub + float(k + 1)) * depth8
            sums = [jnp.zeros((step, cols), jnp.float32)] * 3
            for j in range(start, stop):
                edge_top = jnp.broadcast_to(top_s[r, pl.ds(j, 1), :], (step, cols))
                edge_low = jnp.broadcast_to(low_s[r, pl.ds(j, 1), :], (step, cols))
                shared = jnp.maximum(jnp.minimum(edge_top, ceiling) - jnp.maximum(edge_low, bottom), 0.0)
                for f in range(3):
                    sums[f] = sums[f] + shared * level(j, r, f)
            values = [total * inv8 for total in sums]
            pad_s[r, pl.ds(step + k, step), :] = values[0]
            out[1, pl.ds(2 * k + r, step, stride=2), :] = values[1]
            out[2, pl.ds(2 * k + r, step, stride=2), :] = values[2]
            squares[r].append((values[1] * values[1] * depth8, values[2] * values[2] * depth8))
    copies = [pltpu.make_async_copy(out.at[f], out_h.at[f], sems.at[f]) for f in range(3)]
    copies[1].start()
    copies[2].start()
    stacked = jnp.concatenate(
        [jnp.concatenate([s[i] for s in squares[r]], axis=0) for r in range(2) for i in range(2)], axis=1
    )
    path = running(stacked)
    paths = [path[:, i * cols : (i + 1) * cols] for i in range(4)]
    light = [jnp.zeros((levels, cols), jnp.float32)] * 2
    full = jnp.zeros((1, cols), jnp.float32)
    for b in range(bands):
        a0 = jnp.broadcast_to(powers[pl.ds(b, 1), :], (levels, cols))
        a1 = jnp.broadcast_to(powers[pl.ds(bands + b, 1), :], (levels, cols))
        power = jnp.broadcast_to(powers[pl.ds(2 * bands + b, 1), :], (levels, cols))
        full = full + powers[pl.ds(2 * bands + b, 1), :]
        for r in range(2):
            light[r] = light[r] + power * jnp.exp2(a0 * paths[2 * r] + a1 * paths[2 * r + 1])
    for r in range(2):
        top_s[r] = light[r]
        upper = [jnp.concatenate([full, light[r][: step - 1]], axis=0)]
        upper += [top_s[r, pl.ds(s - 1, step), :] for s in range(step, levels, step)]
        absorbed = (jnp.concatenate(upper, axis=0) - light[r]) * inverse[r]
        heat = absorbed * daylight[r, pl.ds(0, 1), :]
        pad_s[r, pl.ds(0, step), :] = jnp.zeros((step, cols), jnp.float32)
        pad_s[r, pl.ds(step + levels, step), :] = jnp.zeros((step, cols), jnp.float32)
        here = pad_s[r, pl.ds(step, levels), :]
        beneath = pad_s[r, pl.ds(step - 1, levels), :]
        overlying = pad_s[r, pl.ds(step + 1, levels), :]
        cooling = lw_rate * (beneath + overlying - 2.0 * here) - lw_damp * here
        out[0, pl.ds(r, levels, stride=2), :] = here + (heat + cooling)
    copies[0].start()
    for copy in copies:
        copy.wait()


def swapped(x, axis, first):
    size = lax.axis_size(axis)
    pairs = [(i, i + 1) for i in range(first, size - 1, 2)]
    return lax.ppermute(x, axis, [way for i, j in pairs for way in ((i, j), (j, i))])


def core_swap(x):
    size = lax.axis_size("lev")
    return lax.ppermute(x, "lev", [(i, i ^ 1) for i in range(size)])


def between_chips(x, pairs):
    return lax.ppermute(x, "lev", [(2 * a + c, 2 * b + c) for a, b in pairs for c in range(2)])


def local(fields, north, south, east, limiter, thickness, sunlit, absorb, solar_flux):
    _, levels, _, cols = fields.shape
    blocks = cols // LANES
    bands = absorb.shape[1]
    sources = lax.axis_size("lev")
    vmem = pl.BlockSpec(memory_space=pltpu.VMEM)
    smem = pl.BlockSpec(memory_space=pltpu.SMEM)
    hbm = pl.BlockSpec(memory_space=pltpu.HBM)
    params = pltpu.CompilerParams(vmem_limit_bytes=kernel_vmem)
    given = [pltpu.with_memory_space_constraint(block_rows(x), pltpu.HBM) for x in (fields, north, south, limiter, east, thickness)]
    halo = jax.ShapeDtypeStruct((7, levels, cols // 2), jnp.float32)
    near1, near2, far1, far2, *held = pl.pallas_call(
        lambda *refs: pack_body(levels, blocks, *refs),
        out_shape=[halo] * 4 + [jax.ShapeDtypeStruct(x.shape, x.dtype) for x in given],
        in_specs=[hbm] * 6,
        out_specs=[vmem] * 10,
        scratch_shapes=[pltpu.SemaphoreType.DMA((6,))],
        compiler_params=params,
        name="pack",
    )(*given)
    far1 = swapped(far1, "lat", 1)
    near1 = swapped(near1, "lat", 0)
    far2 = swapped(far2, "lat", 1)
    near2 = swapped(near2, "lat", 0)
    powers, daylight = pl.pallas_call(
        lambda *refs: prepare_body(bands, *refs),
        out_shape=(jax.ShapeDtypeStruct((3 * bands, LANES), jnp.float32), jax.ShapeDtypeStruct((2, 8, LANES), jnp.float32)),
        in_specs=[smem] * 3,
        out_specs=(vmem, vmem),
        compiler_params=params,
        cost_estimate=pl.CostEstimate(flops=100000, bytes_accessed=1000000, transcendentals=0),
        name="prepare",
    )(sunlit.reshape(-1), absorb, solar_flux)
    pair = jax.ShapeDtypeStruct((2, 8 * levels, LANES), jnp.float32)

    def advected(part, near, far, *after):
        kept, given_away = pl.pallas_call(
            lambda *refs: advect_body(levels, blocks, part, *refs),
            out_shape=(pair, pair),
            in_specs=[vmem] * (8 + len(after)),
            out_specs=(vmem, vmem),
            compiler_params=params,
        )(*held, near, far, *after)
        swapped_in = core_swap(given_away)
        return pl.pallas_call(
            join_body, out_shape=(pair, pair), in_specs=[vmem] * 2, out_specs=(vmem, vmem), compiler_params=params
        )(kept, swapped_in)

    across1, straight1 = advected(0, near1, far1, powers, daylight)
    third1 = between_chips(across1, ((2, 1), (3, 0)))
    second1 = between_chips(straight1, ((2, 0), (3, 1)))
    beside1 = between_chips(across1, ((0, 1), (1, 0)))
    across2, straight2 = advected(1, near2, far2)
    beside2 = between_chips(across2, ((2, 3), (3, 2)))
    third2 = between_chips(across2, ((0, 3), (1, 2)))
    second2 = between_chips(straight2, ((0, 2), (1, 3)))
    whole = sources * levels
    result = pl.pallas_call(
        lambda *refs: column_body(sources, levels, bands, *refs),
        out_shape=jax.ShapeDtypeStruct((3, whole * 2, LANES), jnp.float32),
        in_specs=[vmem] * 10,
        out_specs=hbm,
        scratch_shapes=[
            pltpu.VMEM((sources, 8 * levels, LANES), jnp.float32),
            pltpu.VMEM((2, whole, LANES), jnp.float32),
            pltpu.VMEM((2, whole, LANES), jnp.float32),
            pltpu.VMEM((2, whole + 16, LANES), jnp.float32),
            pltpu.VMEM((3, whole * 2, LANES), jnp.float32),
            pltpu.SemaphoreType.DMA((3,)),
        ],
        compiler_params=params,
        name="column",
    )(straight1, beside1, second1, third1, straight2, beside2, second2, third2, powers, daylight)
    return result.reshape(3, whole, 2, LANES)


def solution(mesh):
    in_specs = (
        P(None, "lev", "lat", None),
        P("lev", "lat", None),
        P("lev", "lat", None),
        P("lev", "lat", None),
        P("lev", "lat", None),
        P("lev", "lat", None),
        P("lat", "lev"),
        P(),
        P(),
    )
    out_specs = P(None, None, "lat", "lev")

    return jax.shard_map(local, mesh=mesh, in_specs=in_specs, out_specs=out_specs, check_vma=False)
```

```python
import math

import jax
import jax.numpy as jnp
from jax import lax
from jax.experimental import pallas as pl
from jax.experimental.pallas import tpu as pltpu
from jax.sharding import PartitionSpec as P


lw_rate = 0.2
lw_damp = 0.1
LANES = 128
least_thick = 0.5
most_thick = 2.0
kernel_vmem = 8 * 1024 * 1024
log2e = 1.4426950408889634


def block_rows(x):
    lead, (levels, rows, cols) = x.shape[:-3], x.shape[-3:]
    x = x.reshape(*lead, levels, rows, cols // LANES, LANES)
    return jnp.swapaxes(x, -3, -2).reshape(*lead, levels * rows * cols // LANES, LANES)


def row_of(ref, row, levels, blocks, lead=()):
    return jnp.concatenate(
        [ref[(*lead, pl.ds(2 * b + row, levels, stride=2 * blocks), slice(None))] for b in range(blocks)],
        axis=1,
    )


def slope_weights(code):
    wb = jnp.where(code == 1, 1.0, jnp.where(code == 3, 0.5, 0.0))
    wf = jnp.where(code == 2, 1.0, jnp.where(code == 3, 0.5, 0.0))
    return wb, wf


def pack_body(levels, blocks, *refs):
    sources, near, far, held, sems = refs[:6], refs[6], refs[7], refs[8:14], refs[14]
    copies = [pltpu.make_async_copy(src, dst, sems.at[i]) for i, (src, dst) in enumerate(zip(sources, held))]
    for copy in copies:
        copy.start()
    for copy in copies[:4]:
        copy.wait()
    fields, north, south, limiter = held[:4]

    def pack(up, down):
        nc = row_of(north, 1, levels, blocks)
        wb, wf = slope_weights(row_of(limiter, 1, levels, blocks))
        gain = nc * (0.5 * (1.0 - nc))
        up[6] = gain * wf
        sc = row_of(south, 0, levels, blocks)
        vb, vf = slope_weights(row_of(limiter, 0, levels, blocks))
        loss = sc * (0.5 * (1.0 - sc))
        down[6] = loss * vb
        for f in range(3):
            low = row_of(fields, 0, levels, blocks, (f,))
            top = row_of(fields, 1, levels, blocks, (f,))
            step = top - low
            up[f] = top
            up[3 + f] = nc * top + gain * (wb * step - wf * top)
            down[f] = low
            down[3 + f] = sc * low - loss * (vb * low + vf * step)

    odd = lax.rem(lax.axis_index("lat"), 2) == 1
    pl.when(jnp.logical_not(odd))(lambda: pack(near, far))
    pl.when(odd)(lambda: pack(far, near))
    for copy in copies[4:]:
        copy.wait()


def prepare_body(bands, lit, absorb, flux, powers, daylight):
    for b in range(bands):
        powers[pl.ds(b, 1), :] = jnp.full((1, LANES), absorb[0, b] * (-log2e), jnp.float32)
        powers[pl.ds(bands + b, 1), :] = jnp.full((1, LANES), absorb[1, b] * (-log2e), jnp.float32)
        powers[pl.ds(2 * bands + b, 1), :] = jnp.full((1, LANES), flux[b], jnp.float32)
    for r in range(2):
        daylight[r] = jnp.full((8, LANES), lit[r].astype(jnp.float32), jnp.float32)


def advect_body(levels, blocks, *refs):
    core = lax.rem(lax.axis_index("lev"), 2)
    pl.when(core == 0)(lambda: advect(levels, blocks, *refs[:8], refs[10], refs[11]))
    pl.when(core == 1)(lambda: advect(levels, blocks, *refs[:8], refs[11], refs[10]))


def advect(levels, blocks, fields, north, south, limiter, east, thick, near, far, even, odd):
    above_far = lax.rem(lax.axis_index("lat"), 2) == 1

    def below(i):
        return jnp.where(above_far, near[i], far[i])

    def above(i):
        return jnp.where(above_far, far[i], near[i])

    cols = blocks * LANES
    weights, rise_gain, sink_gain, ncs, scs = [], [], [], [], []
    for r in range(2):
        weights.append(slope_weights(row_of(limiter, r, levels, blocks)))
        nc = row_of(north, r, levels, blocks)
        sc = row_of(south, r, levels, blocks)
        ncs.append(nc)
        scs.append(sc)
        rise_gain.append(nc * (0.5 * (1.0 - nc)))
        sink_gain.append(sc * (0.5 * (1.0 - sc)))
    ecs = [row_of(east, r, levels, blocks) for r in range(2)]
    east_gain = [ec * (0.5 * (1.0 - ec)) for ec in ecs]
    for f in range(3):
        rows = [row_of(fields, r, levels, blocks, (f,)) for r in range(2)]
        before = below(f)
        after = above(f)
        diffs = [rows[0] - before, rows[1] - rows[0], after - rows[1]]
        rise, sink, kept = [], [], []
        for r in range(2):
            wb, wf = weights[r]
            slope = wb * diffs[r] + wf * diffs[r + 1]
            rise.append(ncs[r] * rows[r] + rise_gain[r] * slope)
            sink.append(scs[r] * rows[r] - sink_gain[r] * slope)
            step = rows[r] - pltpu.roll(rows[r], 1, 1)
            zonal = wb * step + wf * pltpu.roll(step, cols - 1, 1)
            going = ecs[r] * rows[r] + east_gain[r] * zonal
            kept.append(rows[r] - (going - pltpu.roll(going, 1, 1)))
        from_below = below(3 + f) + below(6) * rows[0]
        from_above = above(3 + f) + above(6) * rows[1]
        first = kept[0] - (rise[0] + sink[0]) + (from_below + sink[1])
        second = kept[1] - (rise[1] + sink[1]) + (rise[0] + from_above)
        for r, value in enumerate((first, second)):
            for b in range(blocks):
                out = (even, odd)[b % 2]
                out[b // 2, pl.ds((r * 4 + f) * levels, levels), :] = value[:, b * LANES : (b + 1) * LANES]
    for r in range(2):
        for b in range(blocks):
            out = (even, odd)[b % 2]
            out[b // 2, pl.ds((r * 4 + 3) * levels, levels), :] = thick[pl.ds(2 * b + r, levels, stride=2 * blocks), :]


def join_body(kept, swapped_in, *out):
    place = lax.axis_index("lev")
    chip, core = lax.shift_right_logical(place, 1), lax.rem(place, 2)
    for q in range(4):
        target = lax.bitwise_xor(chip, q)
        out[q][core] = kept[target]
        out[q][1 - core] = swapped_in[target]


def reach(first, last, levels):
    ratio = most_thick / least_thick
    lo, hi = first / levels, last / levels
    low = levels * lo / (ratio - (ratio - 1.0) * lo)
    high = levels * ratio * hi / (1.0 + (ratio - 1.0) * hi)
    return max(0, math.floor(low) - 1), min(levels, math.ceil(high) + 1)


def column_body(sources, per, bands, own, beside1, second1, third1, beside2, second2, third2, powers, daylight, out_h, got, low_s, top_s, pad_s, out, sems):
    levels = sources * per
    cols = LANES
    chip = lax.shift_right_logical(lax.axis_index("lev"), 1)

    def place(pieces):
        for q, piece in enumerate(pieces):
            source = lax.bitwise_xor(chip, q)
            for c in range(2):
                got[2 * source + c] = piece[c]

    pl.when(chip < 2)(lambda: place((own, beside1, second1, third1)))
    pl.when(chip >= 2)(lambda: place((own, beside2, second2, third2)))
    at_row = lax.broadcasted_iota(jnp.int32, (levels, levels), 0)
    at_col = lax.broadcasted_iota(jnp.int32, (levels, levels), 1)
    triangle = jnp.where(at_row >= at_col, 1.0, 0.0).astype(jnp.bfloat16)

    def running(x):
        total = None
        for _ in range(3):
            part = x.astype(jnp.bfloat16)
            x = x - part.astype(jnp.float32)
            sums = jnp.dot(triangle, part, preferred_element_type=jnp.float32)
            total = sums if total is None else total + sums
        return total

    def piece(s, r, f):
        return got[s, pl.ds((r * 4 + f) * per, per), :]

    def level(j, r, f):
        line = got[j // per, pl.ds((r * 4 + f) * per + j % per, 1), :]
        return jnp.broadcast_to(line, (8, cols))

    thick = jnp.concatenate(
        [jnp.concatenate([piece(s, r, 3) for s in range(sources)], axis=0) for r in range(2)], axis=1
    )
    top = running(thick)
    low = top - thick
    step = 8
    depths, inverse = [], []
    for r in range(2):
        top_s[r] = top[:, r * cols : (r + 1) * cols]
        low_s[r] = low[:, r * cols : (r + 1) * cols]
        depth = top_s[r, pl.ds(levels - 1, 1), :] * (1.0 / levels)
        depths.append(depth)
        inverse.append(1.0 / depth)
    sub = lax.broadcasted_iota(jnp.int32, (step, cols), 0).astype(jnp.float32)
    squares = [[], []]
    for r in range(2):
        depth8 = jnp.broadcast_to(depths[r], (step, cols))
        inv8 = jnp.broadcast_to(inverse[r], (step, cols))
        for k in range(0, levels, step):
            start, stop = reach(k, k + step, levels)
            bottom = (sub + float(k)) * depth8
            ceiling = (sub + float(k + 1)) * depth8
            sums = [jnp.zeros((step, cols), jnp.float32)] * 3
            for j in range(start, stop):
                edge_top = jnp.broadcast_to(top_s[r, pl.ds(j, 1), :], (step, cols))
                edge_low = jnp.broadcast_to(low_s[r, pl.ds(j, 1), :], (step, cols))
                shared = jnp.maximum(jnp.minimum(edge_top, ceiling) - jnp.maximum(edge_low, bottom), 0.0)
                for f in range(3):
                    sums[f] = sums[f] + shared * level(j, r, f)
            values = [total * inv8 for total in sums]
            pad_s[r, pl.ds(step + k, step), :] = values[0]
            out[1, pl.ds(2 * k + r, step, stride=2), :] = values[1]
            out[2, pl.ds(2 * k + r, step, stride=2), :] = values[2]
            squares[r].append((values[1] * values[1] * depth8, values[2] * values[2] * depth8))
    copies = [pltpu.make_async_copy(out.at[f], out_h.at[f], sems.at[f]) for f in range(3)]
    copies[1].start()
    copies[2].start()
    stacked = jnp.concatenate(
        [jnp.concatenate([s[i] for s in squares[r]], axis=0) for r in range(2) for i in range(2)], axis=1
    )
    path = running(stacked)
    paths = [path[:, i * cols : (i + 1) * cols] for i in range(4)]
    light = [jnp.zeros((levels, cols), jnp.float32)] * 2
    full = jnp.zeros((1, cols), jnp.float32)
    for b in range(bands):
        a0 = jnp.broadcast_to(powers[pl.ds(b, 1), :], (levels, cols))
        a1 = jnp.broadcast_to(powers[pl.ds(bands + b, 1), :], (levels, cols))
        power = jnp.broadcast_to(powers[pl.ds(2 * bands + b, 1), :], (levels, cols))
        full = full + powers[pl.ds(2 * bands + b, 1), :]
        for r in range(2):
            light[r] = light[r] + power * jnp.exp2(a0 * paths[2 * r] + a1 * paths[2 * r + 1])
    for r in range(2):
        top_s[r] = light[r]
        upper = [jnp.concatenate([full, light[r][: step - 1]], axis=0)]
        upper += [top_s[r, pl.ds(s - 1, step), :] for s in range(step, levels, step)]
        absorbed = (jnp.concatenate(upper, axis=0) - light[r]) * inverse[r]
        heat = absorbed * daylight[r, pl.ds(0, 1), :]
        pad_s[r, pl.ds(0, step), :] = jnp.zeros((step, cols), jnp.float32)
        pad_s[r, pl.ds(step + levels, step), :] = jnp.zeros((step, cols), jnp.float32)
        here = pad_s[r, pl.ds(step, levels), :]
        beneath = pad_s[r, pl.ds(step - 1, levels), :]
        overlying = pad_s[r, pl.ds(step + 1, levels), :]
        cooling = lw_rate * (beneath + overlying - 2.0 * here) - lw_damp * here
        out[0, pl.ds(r, levels, stride=2), :] = here + (heat + cooling)
    copies[0].start()
    for copy in copies:
        copy.wait()


def swapped(x, axis, first):
    size = lax.axis_size(axis)
    pairs = [(i, i + 1) for i in range(first, size - 1, 2)]
    return lax.ppermute(x, axis, [way for i, j in pairs for way in ((i, j), (j, i))])


def core_swap(x):
    size = lax.axis_size("lev")
    return lax.ppermute(x, "lev", [(i, i ^ 1) for i in range(size)])


def between_chips(x, pairs):
    return lax.ppermute(x, "lev", [(2 * a + c, 2 * b + c) for a, b in pairs for c in range(2)])


def local(fields, north, south, east, limiter, thickness, sunlit, absorb, solar_flux):
    _, levels, _, cols = fields.shape
    blocks = cols // LANES
    bands = absorb.shape[1]
    sources = lax.axis_size("lev")
    vmem = pl.BlockSpec(memory_space=pltpu.VMEM)
    smem = pl.BlockSpec(memory_space=pltpu.SMEM)
    hbm = pl.BlockSpec(memory_space=pltpu.HBM)
    params = pltpu.CompilerParams(vmem_limit_bytes=kernel_vmem)
    given = [pltpu.with_memory_space_constraint(block_rows(x), pltpu.HBM) for x in (fields, north, south, limiter, east, thickness)]
    halo = jax.ShapeDtypeStruct((7, levels, cols), jnp.float32)
    near, far, *held = pl.pallas_call(
        lambda *refs: pack_body(levels, blocks, *refs),
        out_shape=[halo, halo] + [jax.ShapeDtypeStruct(x.shape, x.dtype) for x in given],
        in_specs=[hbm] * 6,
        out_specs=[vmem] * 8,
        scratch_shapes=[pltpu.SemaphoreType.DMA((6,))],
        compiler_params=params,
        name="pack",
    )(*given)
    far = swapped(far, "lat", 1)
    near = swapped(near, "lat", 0)
    powers, daylight = pl.pallas_call(
        lambda *refs: prepare_body(bands, *refs),
        out_shape=(jax.ShapeDtypeStruct((3 * bands, LANES), jnp.float32), jax.ShapeDtypeStruct((2, 8, LANES), jnp.float32)),
        in_specs=[smem] * 3,
        out_specs=(vmem, vmem),
        compiler_params=params,
        cost_estimate=pl.CostEstimate(flops=100000, bytes_accessed=1000000, transcendentals=0),
        name="prepare",
    )(sunlit.reshape(-1), absorb, solar_flux)
    half = jax.ShapeDtypeStruct((sources // 2, 8 * levels, LANES), jnp.float32)
    kept, given_away = pl.pallas_call(
        lambda *refs: advect_body(levels, blocks, *refs),
        out_shape=(half, half),
        in_specs=[vmem] * 10,
        out_specs=(vmem, vmem),
        compiler_params=params,
        name="advect",
    )(*held, near, far, powers, daylight)
    pair = jax.ShapeDtypeStruct((2, 8 * levels, LANES), jnp.float32)
    own, beside, second, third = pl.pallas_call(
        join_body,
        out_shape=[pair] * 4,
        in_specs=[vmem] * 2,
        out_specs=[vmem] * 4,
        compiler_params=params,
        name="join",
    )(kept, core_swap(given_away))
    third1 = between_chips(third, ((2, 1), (3, 0)))
    second1 = between_chips(second, ((2, 0), (3, 1)))
    beside1 = between_chips(beside, ((0, 1), (1, 0)))
    third2 = between_chips(third, ((0, 3), (1, 2)))
    second2 = between_chips(second, ((0, 2), (1, 3)))
    beside2 = between_chips(beside, ((2, 3), (3, 2)))
    whole = sources * levels
    result = pl.pallas_call(
        lambda *refs: column_body(sources, levels, bands, *refs),
        out_shape=jax.ShapeDtypeStruct((3, whole * 2, LANES), jnp.float32),
        in_specs=[vmem] * 9,
        out_specs=hbm,
        scratch_shapes=[
            pltpu.VMEM((sources, 8 * levels, LANES), jnp.float32),
            pltpu.VMEM((2, whole, LANES), jnp.float32),
            pltpu.VMEM((2, whole, LANES), jnp.float32),
            pltpu.VMEM((2, whole + 16, LANES), jnp.float32),
            pltpu.VMEM((3, whole * 2, LANES), jnp.float32),
            pltpu.SemaphoreType.DMA((3,)),
        ],
        compiler_params=params,
        name="column",
    )(own, beside1, second1, third1, beside2, second2, third2, powers, daylight)
    return result.reshape(3, whole, 2, LANES)


def solution(mesh):
    in_specs = (
        P(None, "lev", "lat", None),
        P("lev", "lat", None),
        P("lev", "lat", None),
        P("lev", "lat", None),
        P("lev", "lat", None),
        P("lev", "lat", None),
        P("lat", "lev"),
        P(),
        P(),
    )
    out_specs = P(None, None, "lat", "lev")

    return jax.shard_map(local, mesh=mesh, in_specs=in_specs, out_specs=out_specs, check_vma=False)
```

```python
import math

import jax
import jax.numpy as jnp
from jax import lax
from jax.experimental import pallas as pl
from jax.experimental.pallas import tpu as pltpu
from jax.sharding import PartitionSpec as P


lw_rate = 0.2
lw_damp = 0.1
LANES = 128
least_thick = 0.5
most_thick = 2.0
kernel_vmem = 8 * 1024 * 1024
log2e = 1.4426950408889634


def block_rows(x):
    lead, (levels, rows, cols) = x.shape[:-3], x.shape[-3:]
    x = x.reshape(*lead, levels, rows, cols // LANES, LANES)
    return jnp.swapaxes(x, -3, -2).reshape(*lead, levels * rows * cols // LANES, LANES)


def row_of(ref, row, levels, blocks, lead=()):
    return jnp.concatenate(
        [ref[(*lead, pl.ds(2 * b + row, levels, stride=2 * blocks), slice(None))] for b in range(blocks)],
        axis=1,
    )


def slope_weights(code):
    wb = jnp.where(code == 1, 1.0, jnp.where(code == 3, 0.5, 0.0))
    wf = jnp.where(code == 2, 1.0, jnp.where(code == 3, 0.5, 0.0))
    return wb, wf


def pack_body(levels, blocks, *refs):
    sources, near, far, held, sems = refs[:6], refs[6], refs[7], refs[8:14], refs[14]
    copies = [pltpu.make_async_copy(src, dst, sems.at[i]) for i, (src, dst) in enumerate(zip(sources, held))]
    for copy in copies:
        copy.start()
    for copy in copies[:4]:
        copy.wait()
    fields, north, south, limiter = held[:4]

    def pack(up, down):
        nc = row_of(north, 1, levels, blocks)
        wb, wf = slope_weights(row_of(limiter, 1, levels, blocks))
        gain = nc * (0.5 * (1.0 - nc))
        up[6] = gain * wf
        sc = row_of(south, 0, levels, blocks)
        vb, vf = slope_weights(row_of(limiter, 0, levels, blocks))
        loss = sc * (0.5 * (1.0 - sc))
        down[6] = loss * vb
        for f in range(3):
            low = row_of(fields, 0, levels, blocks, (f,))
            top = row_of(fields, 1, levels, blocks, (f,))
            step = top - low
            up[f] = top
            up[3 + f] = nc * top + gain * (wb * step - wf * top)
            down[f] = low
            down[3 + f] = sc * low - loss * (vb * low + vf * step)

    odd = lax.rem(lax.axis_index("lat"), 2) == 1
    pl.when(jnp.logical_not(odd))(lambda: pack(near, far))
    pl.when(odd)(lambda: pack(far, near))
    for copy in copies[4:]:
        copy.wait()


def prepare_body(bands, lit, absorb, flux, powers, daylight):
    for b in range(bands):
        powers[pl.ds(b, 1), :] = jnp.full((1, LANES), absorb[0, b] * (-log2e), jnp.float32)
        powers[pl.ds(bands + b, 1), :] = jnp.full((1, LANES), absorb[1, b] * (-log2e), jnp.float32)
        powers[pl.ds(2 * bands + b, 1), :] = jnp.full((1, LANES), flux[b], jnp.float32)
    for r in range(2):
        daylight[r] = jnp.full((8, LANES), lit[r].astype(jnp.float32), jnp.float32)


def advect_body(levels, blocks, *refs):
    core = lax.rem(lax.axis_index("lev"), 2)
    pl.when(core == 0)(lambda: advect(levels, blocks, *refs[:8], refs[10], refs[11]))
    pl.when(core == 1)(lambda: advect(levels, blocks, *refs[:8], refs[11], refs[10]))


def advect(levels, blocks, fields, north, south, limiter, east, thick, near, far, even, odd):
    above_far = lax.rem(lax.axis_index("lat"), 2) == 1

    def below(i):
        return jnp.where(above_far, near[i], far[i])

    def above(i):
        return jnp.where(above_far, far[i], near[i])

    cols = blocks * LANES
    weights, rise_gain, sink_gain, ncs, scs = [], [], [], [], []
    for r in range(2):
        weights.append(slope_weights(row_of(limiter, r, levels, blocks)))
        nc = row_of(north, r, levels, blocks)
        sc = row_of(south, r, levels, blocks)
        ncs.append(nc)
        scs.append(sc)
        rise_gain.append(nc * (0.5 * (1.0 - nc)))
        sink_gain.append(sc * (0.5 * (1.0 - sc)))
    ecs = [row_of(east, r, levels, blocks) for r in range(2)]
    east_gain = [ec * (0.5 * (1.0 - ec)) for ec in ecs]
    for f in range(3):
        rows = [row_of(fields, r, levels, blocks, (f,)) for r in range(2)]
        before = below(f)
        after = above(f)
        diffs = [rows[0] - before, rows[1] - rows[0], after - rows[1]]
        rise, sink, kept = [], [], []
        for r in range(2):
            wb, wf = weights[r]
            slope = wb * diffs[r] + wf * diffs[r + 1]
            rise.append(ncs[r] * rows[r] + rise_gain[r] * slope)
            sink.append(scs[r] * rows[r] - sink_gain[r] * slope)
            step = rows[r] - pltpu.roll(rows[r], 1, 1)
            zonal = wb * step + wf * pltpu.roll(step, cols - 1, 1)
            going = ecs[r] * rows[r] + east_gain[r] * zonal
            kept.append(rows[r] - (going - pltpu.roll(going, 1, 1)))
        from_below = below(3 + f) + below(6) * rows[0]
        from_above = above(3 + f) + above(6) * rows[1]
        first = kept[0] - (rise[0] + sink[0]) + (from_below + sink[1])
        second = kept[1] - (rise[1] + sink[1]) + (rise[0] + from_above)
        for r, value in enumerate((first, second)):
            for b in range(blocks):
                out = (even, odd)[b % 2]
                out[b // 2, pl.ds((r * 4 + f) * levels, levels), :] = value[:, b * LANES : (b + 1) * LANES]
    for r in range(2):
        for b in range(blocks):
            out = (even, odd)[b % 2]
            out[b // 2, pl.ds((r * 4 + 3) * levels, levels), :] = thick[pl.ds(2 * b + r, levels, stride=2 * blocks), :]


def join_body(kept, swapped_in, *out):
    place = lax.axis_index("lev")
    chip, core = lax.shift_right_logical(place, 1), lax.rem(place, 2)
    for q in range(4):
        target = lax.bitwise_xor(chip, q)
        out[q][core] = kept[target]
        out[q][1 - core] = swapped_in[target]


def reach(first, last, levels):
    ratio = most_thick / least_thick
    lo, hi = first / levels, last / levels
    low = levels * lo / (ratio - (ratio - 1.0) * lo)
    high = levels * ratio * hi / (1.0 + (ratio - 1.0) * hi)
    return max(0, math.floor(low) - 1), min(levels, math.ceil(high) + 1)


def column_body(upper, *refs):
    chip = lax.shift_right_logical(lax.axis_index("lev"), 1)
    pl.when((chip >= 2) if upper else (chip < 2))(lambda: columns(chip, *refs))


def columns(chip, sources, per, bands, own, beside, second, third, powers, daylight, out_h, got, low_s, top_s, pad_s, out, sems):
    levels = sources * per
    cols = LANES
    for q, piece in enumerate((own, beside, second, third)):
        source = lax.bitwise_xor(chip, q)
        for c in range(2):
            got[2 * source + c] = piece[c]
    at_row = lax.broadcasted_iota(jnp.int32, (levels, levels), 0)
    at_col = lax.broadcasted_iota(jnp.int32, (levels, levels), 1)
    triangle = jnp.where(at_row >= at_col, 1.0, 0.0).astype(jnp.bfloat16)

    def running(x):
        total = None
        for _ in range(3):
            part = x.astype(jnp.bfloat16)
            x = x - part.astype(jnp.float32)
            sums = jnp.dot(triangle, part, preferred_element_type=jnp.float32)
            total = sums if total is None else total + sums
        return total

    def part_of(s, r, f):
        return got[s, pl.ds((r * 4 + f) * per, per), :]

    def level(j, r, f):
        line = got[j // per, pl.ds((r * 4 + f) * per + j % per, 1), :]
        return jnp.broadcast_to(line, (8, cols))

    thick = jnp.concatenate(
        [jnp.concatenate([part_of(s, r, 3) for s in range(sources)], axis=0) for r in range(2)], axis=1
    )
    top = running(thick)
    low = top - thick
    step = 8
    depths, inverse = [], []
    for r in range(2):
        top_s[r] = top[:, r * cols : (r + 1) * cols]
        low_s[r] = low[:, r * cols : (r + 1) * cols]
        depth = top_s[r, pl.ds(levels - 1, 1), :] * (1.0 / levels)
        depths.append(depth)
        inverse.append(1.0 / depth)
    sub = lax.broadcasted_iota(jnp.int32, (step, cols), 0).astype(jnp.float32)
    squares = [[], []]
    for r in range(2):
        depth8 = jnp.broadcast_to(depths[r], (step, cols))
        inv8 = jnp.broadcast_to(inverse[r], (step, cols))
        for k in range(0, levels, step):
            start, stop = reach(k, k + step, levels)
            bottom = (sub + float(k)) * depth8
            ceiling = (sub + float(k + 1)) * depth8
            sums = [jnp.zeros((step, cols), jnp.float32)] * 3
            for j in range(start, stop):
                edge_top = jnp.broadcast_to(top_s[r, pl.ds(j, 1), :], (step, cols))
                edge_low = jnp.broadcast_to(low_s[r, pl.ds(j, 1), :], (step, cols))
                shared = jnp.maximum(jnp.minimum(edge_top, ceiling) - jnp.maximum(edge_low, bottom), 0.0)
                for f in range(3):
                    sums[f] = sums[f] + shared * level(j, r, f)
            values = [total * inv8 for total in sums]
            pad_s[r, pl.ds(step + k, step), :] = values[0]
            out[1, pl.ds(2 * k + r, step, stride=2), :] = values[1]
            out[2, pl.ds(2 * k + r, step, stride=2), :] = values[2]
            squares[r].append((values[1] * values[1] * depth8, values[2] * values[2] * depth8))
    copies = [pltpu.make_async_copy(out.at[f], out_h.at[f], sems.at[f]) for f in range(3)]
    copies[1].start()
    copies[2].start()
    stacked = jnp.concatenate(
        [jnp.concatenate([s[i] for s in squares[r]], axis=0) for r in range(2) for i in range(2)], axis=1
    )
    path = running(stacked)
    paths = [path[:, i * cols : (i + 1) * cols] for i in range(4)]
    light = [jnp.zeros((levels, cols), jnp.float32)] * 2
    full = jnp.zeros((1, cols), jnp.float32)
    for b in range(bands):
        a0 = jnp.broadcast_to(powers[pl.ds(b, 1), :], (levels, cols))
        a1 = jnp.broadcast_to(powers[pl.ds(bands + b, 1), :], (levels, cols))
        power = jnp.broadcast_to(powers[pl.ds(2 * bands + b, 1), :], (levels, cols))
        full = full + powers[pl.ds(2 * bands + b, 1), :]
        for r in range(2):
            light[r] = light[r] + power * jnp.exp2(a0 * paths[2 * r] + a1 * paths[2 * r + 1])
    for r in range(2):
        top_s[r] = light[r]
        upper = [jnp.concatenate([full, light[r][: step - 1]], axis=0)]
        upper += [top_s[r, pl.ds(s - 1, step), :] for s in range(step, levels, step)]
        absorbed = (jnp.concatenate(upper, axis=0) - light[r]) * inverse[r]
        heat = absorbed * daylight[r, pl.ds(0, 1), :]
        pad_s[r, pl.ds(0, step), :] = jnp.zeros((step, cols), jnp.float32)
        pad_s[r, pl.ds(step + levels, step), :] = jnp.zeros((step, cols), jnp.float32)
        here = pad_s[r, pl.ds(step, levels), :]
        beneath = pad_s[r, pl.ds(step - 1, levels), :]
        overlying = pad_s[r, pl.ds(step + 1, levels), :]
        cooling = lw_rate * (beneath + overlying - 2.0 * here) - lw_damp * here
        out[0, pl.ds(r, levels, stride=2), :] = here + (heat + cooling)
    copies[0].start()
    for copy in copies:
        copy.wait()


def swapped(x, axis, first):
    size = lax.axis_size(axis)
    pairs = [(i, i + 1) for i in range(first, size - 1, 2)]
    return lax.ppermute(x, axis, [way for i, j in pairs for way in ((i, j), (j, i))])


def core_swap(x):
    size = lax.axis_size("lev")
    return lax.ppermute(x, "lev", [(i, i ^ 1) for i in range(size)])


def between_chips(x, pairs):
    return lax.ppermute(x, "lev", [(2 * a + c, 2 * b + c) for a, b in pairs for c in range(2)])


def local(fields, north, south, east, limiter, thickness, sunlit, absorb, solar_flux):
    _, levels, _, cols = fields.shape
    blocks = cols // LANES
    bands = absorb.shape[1]
    sources = lax.axis_size("lev")
    vmem = pl.BlockSpec(memory_space=pltpu.VMEM)
    smem = pl.BlockSpec(memory_space=pltpu.SMEM)
    hbm = pl.BlockSpec(memory_space=pltpu.HBM)
    params = pltpu.CompilerParams(vmem_limit_bytes=kernel_vmem)
    given = [pltpu.with_memory_space_constraint(block_rows(x), pltpu.HBM) for x in (fields, north, south, limiter, east, thickness)]
    halo = jax.ShapeDtypeStruct((7, levels, cols), jnp.float32)
    near, far, *held = pl.pallas_call(
        lambda *refs: pack_body(levels, blocks, *refs),
        out_shape=[halo, halo] + [jax.ShapeDtypeStruct(x.shape, x.dtype) for x in given],
        in_specs=[hbm] * 6,
        out_specs=[vmem] * 8,
        scratch_shapes=[pltpu.SemaphoreType.DMA((6,))],
        compiler_params=params,
        name="pack",
    )(*given)
    far = swapped(far, "lat", 1)
    near = swapped(near, "lat", 0)
    powers, daylight = pl.pallas_call(
        lambda *refs: prepare_body(bands, *refs),
        out_shape=(jax.ShapeDtypeStruct((3 * bands, LANES), jnp.float32), jax.ShapeDtypeStruct((2, 8, LANES), jnp.float32)),
        in_specs=[smem] * 3,
        out_specs=(vmem, vmem),
        compiler_params=params,
        cost_estimate=pl.CostEstimate(flops=100000, bytes_accessed=1000000, transcendentals=0),
        name="prepare",
    )(sunlit.reshape(-1), absorb, solar_flux)
    half = jax.ShapeDtypeStruct((sources // 2, 8 * levels, LANES), jnp.float32)
    kept, given_away = pl.pallas_call(
        lambda *refs: advect_body(levels, blocks, *refs),
        out_shape=(half, half),
        in_specs=[vmem] * 10,
        out_specs=(vmem, vmem),
        compiler_params=params,
        name="advect",
    )(*held, near, far, powers, daylight)
    pair = jax.ShapeDtypeStruct((2, 8 * levels, LANES), jnp.float32)
    own, beside, second, third = pl.pallas_call(
        join_body,
        out_shape=[pair] * 4,
        in_specs=[vmem] * 2,
        out_specs=[vmem] * 4,
        compiler_params=params,
        name="join",
    )(kept, core_swap(given_away))
    third1 = between_chips(third, ((2, 1), (3, 0)))
    second1 = between_chips(second, ((2, 0), (3, 1)))
    beside1 = between_chips(beside, ((0, 1), (1, 0)))
    third2 = between_chips(third, ((0, 3), (1, 2)))
    second2 = between_chips(second, ((0, 2), (1, 3)))
    beside2 = between_chips(beside, ((2, 3), (3, 2)))
    whole = sources * levels
    shape = jax.ShapeDtypeStruct((3, whole * 2, LANES), jnp.float32)
    scratch = [
        pltpu.VMEM((sources, 8 * levels, LANES), jnp.float32),
        pltpu.VMEM((2, whole, LANES), jnp.float32),
        pltpu.VMEM((2, whole, LANES), jnp.float32),
        pltpu.VMEM((2, whole + 16, LANES), jnp.float32),
        pltpu.VMEM((3, whole * 2, LANES), jnp.float32),
        pltpu.SemaphoreType.DMA((3,)),
    ]
    result = pl.pallas_call(
        lambda *refs: column_body(False, sources, levels, bands, *refs),
        out_shape=shape,
        in_specs=[vmem] * 6,
        out_specs=hbm,
        scratch_shapes=scratch,
        compiler_params=params,
        name="column_lower",
    )(own, beside1, second1, third1, powers, daylight)
    result = pl.pallas_call(
        lambda *refs: column_body(True, sources, levels, bands, *refs[1:]),
        out_shape=shape,
        in_specs=[hbm] + [vmem] * 6,
        out_specs=hbm,
        input_output_aliases={0: 0},
        scratch_shapes=scratch,
        compiler_params=params,
        name="column_upper",
    )(result, own, beside2, second2, third2, powers, daylight)
    return result.reshape(3, whole, 2, LANES)


def solution(mesh):
    in_specs = (
        P(None, "lev", "lat", None),
        P("lev", "lat", None),
        P("lev", "lat", None),
        P("lev", "lat", None),
        P("lev", "lat", None),
        P("lev", "lat", None),
        P("lat", "lev"),
        P(),
        P(),
    )
    out_specs = P(None, None, "lat", "lev")

    return jax.shard_map(local, mesh=mesh, in_specs=in_specs, out_specs=out_specs, check_vma=False)
```
